128 devices in a mesh: segment: 2 (over core), seq: 32 (over z_lo, y, x), mp: 2 (over z_hi).
Axes of the slice: x: 4, y: 4, z: 4 (z_hi: 2, z_lo: 2; z = z_hi * 2 + z_lo), core: 2. Of those that a mesh axis runs over, the one named last changes fastest.
Arguments:
- inputs: bfloat16 [65536, 512], P('seq', 'mp'), may hold values from -6 to 6
- cotangent: bfloat16 [65536, 512], P('seq', 'mp'), may hold values from -0.375 to 0.375
- gate_gain: float32 [2, 512], P('segment', 'mp'), may hold values from 0.3 to 3
- key_gain: float32 [2, 512], P('segment', 'mp'), may hold values from 0.3 to 3
- first_factor: bfloat16 [2, 256, 256, 256], P('segment', 'seq'), may hold values from -0.375 to 0.375
- second_factor: bfloat16 [2, 256, 256, 256], P('segment', 'seq'), may hold values from -0.375 to 0.375
- up_first: bfloat16 [2, 4, 128, 128], P('segment', 'mp'), may hold values from -0.5 to 0.5
- up_second: bfloat16 [2, 4, 128, 512], P('segment', 'mp'), may hold values from -0.5 to 0.5
- down_first: bfloat16 [2, 4, 512, 128], P('segment', 'mp'), may hold values from -0.25 to 0.25
- down_second_weight: bfloat16 [2, 4, 128, 128], P('segment', 'mp'), may hold values from -0.5 to 0.5
Outputs:
- grad_first: float32 [2, 256, 256, 256], P('segment', 'seq', 'mp')
- grad_second: float32 [2, 256, 256, 256], P('segment', 'seq', 'mp')
The draws below stay inside these ranges and needn't reach their ends.
All inputs are finite; a program needn't handle non-finite values.
Results may differ from the reference program's by a relative error of at most 0.024.
Values may be sent and summed in bfloat16 or wider, within the bound.
No kernel may reach another device: no remote copies, remote signals or barrier semaphores. Data moves between devices by JAX's collectives and lax.ppermute only.
A program may use at most 128 MiB of HBM per device.

```python
import math
import jax
import jax.numpy as jnp

D = 512
BLOCK = 256
NBLK = 4
LENGTH = 65536
BW = 128
HB = 512
SEGMENTS = 2


def block_levels(key, shape, shards, smallest, high):
    gain = 1.0
    for dim, parts in shards:
        steps = jax.random.uniform(jax.random.fold_in(jax.random.fold_in(key, 6), dim), (parts,), jnp.float32, smallest / len(shards), high / len(shards))
        gain = gain * jnp.repeat(jnp.exp(steps), shape[dim] // parts).reshape((-1,) + (1,) * (len(shape) - 1 - dim))
    return gain


def noise(rng, shape, width, bound, pieces=(), dtype=jnp.bfloat16):
    level = block_levels(rng, shape, pieces, -0.22, 0.18) if pieces else 1.0
    array = jax.random.normal(rng, shape, jnp.float32) * width * level
    return jnp.minimum(jnp.maximum(array, -bound), bound).astype(dtype)


def setup_inputs(seed: int = 0) -> dict:
    key_of = jax.random.split(jax.random.key(seed), 11)
    return {
        "inputs": noise(key_of[0], (LENGTH, D), 1.0, 6.0, ((0, 32), (1, 2))),
        "cotangent": noise(key_of[1], (LENGTH, D), 0.0625, 0.375, ((0, 32), (1, 2))),
        "gate_gain": jnp.clip(jnp.exp(math.log(3.0) - 2.3025851 * jax.random.uniform(key_of[2], (SEGMENTS, D), jnp.float32) ** block_levels(key_of[2], (SEGMENTS, D), ((0, 2), (1, 2)), -0.2, 0.2)), 0.3, 3.0),
        "key_gain": jnp.clip(jnp.exp(math.log(3.0) - 2.3025851 * jax.random.uniform(key_of[3], (SEGMENTS, D), jnp.float32) ** block_levels(key_of[3], (SEGMENTS, D), ((0, 2), (1, 2)), -0.2, 0.2)), 0.3, 3.0),
        "first_factor": noise(key_of[4], (SEGMENTS, BLOCK, BLOCK, BLOCK), BLOCK ** -0.5, 0.375, ((0, 2), (1, 32))),
        "second_factor": noise(key_of[5], (SEGMENTS, BLOCK, BLOCK, BLOCK), BLOCK ** -0.5, 0.375, ((0, 2), (1, 32))),
        "up_first": noise(key_of[6], (SEGMENTS, NBLK, BW, BW), BW ** -0.5, 0.5, ((0, 2), (1, 2))),
        "up_second": noise(key_of[7], (SEGMENTS, NBLK, BW, HB), BW ** -0.5, 0.5, ((0, 2), (1, 2))),
        "down_first": noise(key_of[8], (SEGMENTS, NBLK, HB, BW), HB ** -0.5, 0.25, ((0, 2), (1, 2))),
        "down_second_weight": noise(key_of[9], (SEGMENTS, NBLK, BW, BW), BW ** -0.5, 0.5, ((0, 2), (1, 2))),
    }


def sigmoid_slope(values):
    logistic = jax.nn.sigmoid(values)
    return logistic * (1.0 + values * (1.0 - logistic))


def layer_forward(rows_in, gate_gain, key_gain, first_block, second_block, up_first, up_second, down_first, down_second_weight):
    sequence_length = rows_in.shape[0]
    model_width = rows_in.shape[1]
    block_count = up_first.shape[0]
    block_column_width = up_first.shape[1]
    sub_width = block_column_width // block_count
    rows_grid = rows_in.reshape(BLOCK, BLOCK, model_width).astype(jnp.float32)
    scaled = (rows_grid * key_gain).astype(jnp.bfloat16)
    mixed_rows = jnp.einsum('aoi,aic->aoc', first_block.astype(jnp.float32), scaled.astype(jnp.float32)).astype(jnp.bfloat16)
    turned = jnp.einsum('boi,ibc->obc', second_block.astype(jnp.float32), mixed_rows.astype(jnp.float32)).astype(jnp.bfloat16)
    gate_pre = rows_grid * gate_gain
    hidden_rows = (rows_grid + jax.nn.silu(gate_pre) * turned.astype(jnp.float32)).astype(jnp.bfloat16)
    hidden_rows = hidden_rows.reshape(sequence_length, block_count, block_column_width)
    up_grid = up_first.reshape(block_count, block_column_width, block_count, sub_width).astype(jnp.float32)
    permuted = jnp.einsum('tki,kijc->tjkc', hidden_rows.astype(jnp.float32), up_grid).astype(jnp.bfloat16)
    permuted = permuted.reshape(sequence_length, block_count, block_column_width)
    preact = jnp.einsum('tjq,jqe->tje', permuted.astype(jnp.float32), up_second.astype(jnp.float32))
    active = jax.nn.silu(preact).astype(jnp.bfloat16)
    down_grid = down_first.reshape(block_count, down_first.shape[1], block_count, sub_width).astype(jnp.float32)
    folded_rows = jnp.einsum('tje,jemc->tmjc', active.astype(jnp.float32), down_grid).astype(jnp.bfloat16)
    folded_rows = folded_rows.reshape(sequence_length, block_count, block_column_width)
    output_portion = jnp.einsum('xds,dsl->xdl', folded_rows.astype(jnp.float32), down_second_weight.astype(jnp.float32))
    result = (hidden_rows.astype(jnp.float32) + output_portion).reshape(sequence_length, model_width).astype(jnp.bfloat16)
    return result, (rows_grid, scaled, mixed_rows, turned, preact)


def layer_backward(cot_rows, kept_state, gate_gain, key_gain, first_block, second_block, up_first, up_second, down_first, down_second_weight):
    rows_grid, scaled, mixed_rows, turned, preact = kept_state
    sequence_length = cot_rows.shape[0]
    model_width = cot_rows.shape[1]
    block_count = up_first.shape[0]
    block_column_width = up_first.shape[1]
    sub_width = block_column_width // block_count
    up_grid = up_first.reshape(block_count, block_column_width, block_count, sub_width).astype(jnp.float32)
    down_grid = down_first.reshape(block_count, down_first.shape[1], block_count, sub_width).astype(jnp.float32)
    cotangent_float = cot_rows.astype(jnp.float32)
    backward_folded_rows = jnp.einsum('hsd,sad->hsa', cotangent_float.reshape(sequence_length, block_count, block_column_width), down_second_weight.astype(jnp.float32)).astype(jnp.bfloat16)
    back_grid = backward_folded_rows.reshape(sequence_length, block_count, block_count, sub_width).astype(jnp.float32)
    back_active = jnp.einsum('tmjc,jemc->tje', back_grid, down_grid)
    back_preact = (back_active * sigmoid_slope(preact)).astype(jnp.bfloat16)
    back_perm = jnp.einsum('tje,jqe->tjq', back_preact.astype(jnp.float32), up_second.astype(jnp.float32)).astype(jnp.bfloat16)
    back_perm_grid = back_perm.reshape(sequence_length, block_count, block_count, sub_width).astype(jnp.float32)
    back_ffn = jnp.einsum('tjkc,kijc->tki', back_perm_grid, up_grid).reshape(BLOCK, BLOCK, model_width)
    back_hidden = cotangent_float.reshape(BLOCK, BLOCK, model_width) + back_ffn
    gate_pre = rows_grid * gate_gain
    back_turned = (back_hidden * jax.nn.silu(gate_pre)).astype(jnp.bfloat16)
    second_grad = jnp.einsum('obc,ibc->boi', back_turned.astype(jnp.float32), mixed_rows.astype(jnp.float32))
    back_mixed = jnp.einsum('boi,obc->ibc', second_block.astype(jnp.float32), back_turned.astype(jnp.float32)).astype(jnp.bfloat16)
    first_grad = jnp.einsum('aoc,aic->aoi', back_mixed.astype(jnp.float32), scaled.astype(jnp.float32))
    back_scaled = jnp.einsum('aoi,aoc->aic', first_block.astype(jnp.float32), back_mixed.astype(jnp.float32))
    back_inputs = back_hidden + back_hidden * turned.astype(jnp.float32) * sigmoid_slope(gate_pre) * gate_gain + back_scaled * key_gain
    back_inputs = back_inputs.reshape(sequence_length, model_width).astype(jnp.bfloat16)
    return back_inputs, first_grad, second_grad


def segment_weights(segment_index, gate_gain, key_gain, first_factor, second_factor, up_first, up_second, down_first, down_second_weight):
    return (gate_gain[segment_index], key_gain[segment_index], first_factor[segment_index], second_factor[segment_index],
            up_first[segment_index], up_second[segment_index], down_first[segment_index], down_second_weight[segment_index])


def reference(inputs, cotangent, gate_gain, key_gain, first_factor, second_factor, up_first, up_second, down_first, down_second_weight):
    lower = segment_weights(0, gate_gain, key_gain, first_factor, second_factor, up_first, up_second, down_first, down_second_weight)
    upper = segment_weights(1, gate_gain, key_gain, first_factor, second_factor, up_first, up_second, down_first, down_second_weight)
    middle, kept_lower = layer_forward(inputs, *lower)
    unused_out, kept_upper = layer_forward(middle, *upper)
    passed, first_upper, second_upper = layer_backward(cotangent, kept_upper, *upper)
    ignored, first_lower, second_lower = layer_backward(passed, kept_lower, *lower)
    return jnp.stack([first_lower, first_upper]), jnp.stack([second_lower, second_upper])
```

```python
import functools

import jax
import jax.numpy as jnp
from jax import lax
from jax.experimental import pallas as pl
from jax.experimental.pallas import tpu as pltpu
from jax.sharding import PartitionSpec as P

ROWS_ORDER = ("seq", "segment", "mp")
QUARTER_ORDER = ("mp", "seq", "segment")
BF = jnp.bfloat16
F32 = jnp.float32
MSG = (2048, 128)


def exchange(message, order):
    return lax.all_to_all(message, order, split_axis=0, concat_axis=0, tiled=True)


def swap(value, axis):
    return lax.ppermute(value, axis, [(0, 1), (1, 0)])


def pick(flag, when_zero, when_one):
    return jnp.where(flag == 0, when_zero, when_one)


def dot(a, b):
    return jnp.dot(a, b, preferred_element_type=F32)


def dot_nt(a, b):
    return lax.dot_general(a, b, (((1,), (1,)), ((), ())), preferred_element_type=F32)


def sigmoid(v):
    return 0.5 * jnp.tanh(0.5 * v) + 0.5


def slope(v):
    s = sigmoid(v)
    return s * (1.0 + v * (1.0 - s))


def call(body, name, outs, scratch, args, smem=0, flops=10**8):
    specs = [pl.BlockSpec(memory_space=pltpu.SMEM)] * smem
    specs += [pl.BlockSpec(memory_space=pltpu.VMEM)] * (len(args) - smem)
    out_shape = tuple(jax.ShapeDtypeStruct(s, d) for s, d in outs)
    moved = sum(a.size * a.dtype.itemsize for a in args) + sum(
        o.size * o.dtype.itemsize for o in out_shape
    )
    return pl.pallas_call(
        body,
        out_shape=out_shape,
        in_specs=specs,
        out_specs=tuple(pl.BlockSpec(memory_space=pltpu.VMEM) for _ in outs),
        scratch_shapes=[pltpu.VMEM(s, d) for s, d in scratch],
        compiler_params=pltpu.CompilerParams(vmem_limit_bytes=40 * 2**20),
        cost_estimate=pl.CostEstimate(flops=flops, bytes_accessed=moved, transcendentals=0),
        name=name,
    )(*args)


def pack_quarter(values, a, out, temp):
    for h in range(2):
        temp[...] = values[:, h * 128 : (h + 1) * 128]
        for mm in range(2):
            for oo in range(2):
                out[pl.ds(mm * 1024 + a * 4 + oo * 2 + h, 64, stride=16), :] = temp[
                    pl.ds(mm * 2 + oo, 64, stride=4), :
                ]


def unpack_quarter(source, oo):
    parts = [
        source[pl.ds(mm * 1024 + oo * 2 + h, 256, stride=4), :] for mm in range(2) for h in range(2)
    ]
    return jnp.concatenate(parts, axis=1)


def pack_cols(values, oo, out):
    for cq in range(4):
        out[pl.ds(oo * 4 + cq, 256, stride=8), :] = values[:, cq * 128 : (cq + 1) * 128]


def unpack_cols(source, oo):
    return jnp.concatenate(
        [source[pl.ds(oo * 4 + cq, 256, stride=8), :] for cq in range(4)], axis=1
    )


def pack_rows(values, a2, out, temp):
    for cq in range(4):
        temp[...] = values[:, cq * 128 : (cq + 1) * 128]
        for oo in range(2):
            out[pl.ds(a2 * 8 + oo * 4 + cq, 128, stride=16), :] = temp[pl.ds(oo, 128, stride=2), :]


def unpack_rows(source, a2, temp):
    for cq in range(4):
        for oo in range(2):
            temp[cq, pl.ds(oo, 128, stride=2), :] = source[
                pl.ds(a2 * 8 + oo * 4 + cq, 128, stride=16), :
            ]
    return jnp.concatenate([temp[cq] for cq in range(4)], axis=1)


def pack_body(g_ref, x_ref, out_ref, packed, temp):
    g = g_ref[0]
    for a in range(4):
        pack_quarter(x_ref[4 * g + a].astype(F32), a, packed, temp)
    out_ref[...] = packed[...].astype(BF)


def first_rows_body(g_ref, x_ref, mine_ref, got_ref, key_ref, out_ref, packed, temp):
    g = g_ref[0]
    for a in range(4):
        scaled = (x_ref[4 * g + a].astype(F32) * key_ref[...]).astype(BF)
        factor = jnp.where(g == 0, mine_ref[a], got_ref[a])
        pack_quarter(dot(factor, scaled), a, packed, temp)
    out_ref[...] = packed[...].astype(BF)


def prepare_body(up_ref, down_ref, u_ref, v_ref):
    rho = lax.broadcasted_iota(jnp.int32, (128, 512), 0)
    gam = lax.broadcasted_iota(jnp.int32, (128, 512), 1)
    same = (gam // 128) * 32 + gam % 32 == rho
    for k in range(4):
        place = jnp.where(same & ((gam // 32) % 4 == k), 1.0, 0.0).astype(BF)
        u_ref[k * 128 : (k + 1) * 128, :] = dot(up_ref[k], place).astype(BF)
        spread = lax.dot_general(
            place, down_ref[k], (((0,), (0,)), ((), ())), preferred_element_type=F32
        )
        v_ref[:, k * 128 : (k + 1) * 128] = spread.astype(BF)


def forward_cols_body(
    mixed_msg, x_msg, factor, gate, key, u, v, up2, down1,
    out_msg, mixed_out, x_out, hidden_out, turned_out, middle_out,
    wide, wide_x,
):
    wide[...] = mixed_msg[...].astype(F32)
    wide_x[...] = x_msg[...].astype(F32)
    scaled = []
    for oo in range(2):
        part = slice(oo * 256, (oo + 1) * 256)
        mixed = unpack_quarter(wide, oo).astype(BF)
        x = unpack_quarter(wide_x, oo)
        turned = dot(factor[oo], mixed).astype(BF)
        pre = x * gate[...]
        hidden = (x + pre * sigmoid(pre) * turned.astype(F32)).astype(BF)
        mixed_out[part, :] = mixed
        x_out[part, :] = x.astype(BF)
        hidden_out[part, :] = hidden
        turned_out[part, :] = turned
        permuted = dot(hidden, u[...]).astype(BF)
        folds = []
        for j in range(4):
            preact = dot(permuted[:, j * 128 : (j + 1) * 128], up2[j])
            active = (preact * sigmoid(preact)).astype(BF)
            folds.append(dot(active, down1[j]).astype(BF))
        out = dot(jnp.concatenate(folds, axis=1), v[...])
        middle = (hidden.astype(F32) + out).astype(BF)
        middle_out[part, :] = middle
        scaled.append((middle.astype(F32) * key[...]).astype(BF).astype(F32))
    for oo in range(2):
        pack_cols(scaled[oo], oo, wide)
    out_msg[...] = wide[...].astype(BF)


def rows_body(msg, factor, scale, out_msg, saved, wide, packed, temp, temp4):
    wide[...] = msg[...].astype(F32)
    for a2 in range(2):
        values = unpack_rows(wide, a2, temp4).astype(BF)
        saved[a2] = values
        result = dot(factor[a2], values) * scale[...]
        pack_rows(result, a2, packed, temp)
    out_msg[...] = packed[...].astype(BF)


def last_rows_body(msg, x_ref, key, grad, wide, temp4):
    wide[...] = msg[...].astype(F32)
    for a2 in range(2):
        values = unpack_rows(wide, a2, temp4).astype(BF)
        scaled = (x_ref[a2].astype(F32) * key[...]).astype(BF)
        grad[a2] = dot_nt(values, scaled).astype(BF)


def ffn_back(cot, hidden, u, v, up2, down1):
    permuted = dot(hidden, u[...]).astype(BF)
    fold = dot_nt(cot, v[...]).astype(BF)
    perms = []
    for j in range(4):
        block = slice(j * 128, (j + 1) * 128)
        preact = dot(permuted[:, block], up2[j])
        back_active = dot_nt(fold[:, block], down1[j])
        back_preact = (back_active * slope(preact)).astype(BF)
        perms.append(dot_nt(back_preact, up2[j]).astype(BF))
    return cot.astype(F32) + dot_nt(jnp.concatenate(perms, axis=1), u[...])


def upper_cols_body(
    mixed_msg, cot_msg, x_ref, factor, factor_t, gate, u, v, up2, down1,
    out_msg, mixed_out, back_turned_out, direct_out,
    wide, wide_c, packed,
):
    wide[...] = mixed_msg[...].astype(F32)
    wide_c[...] = cot_msg[...].astype(F32)
    for oo in range(2):
        part = slice(oo * 256, (oo + 1) * 256)
        mixed = unpack_cols(wide, oo).astype(BF)
        cot = unpack_quarter(wide_c, oo).astype(BF)
        mixed_out[part, :] = mixed
        x = x_ref[part, :].astype(F32)
        turned = dot(factor[oo], mixed).astype(BF).astype(F32)
        pre = x * gate[...]
        logistic = sigmoid(pre)
        gated = pre * logistic
        hidden = (x + gated * turned).astype(BF)
        back_hidden = ffn_back(cot, hidden, u, v, up2, down1)
        back_turned = (back_hidden * gated).astype(BF)
        back_turned_out[part, :] = back_turned
        pack_cols(dot(factor_t[oo], back_turned), oo, packed)
        gate_slope = logistic * (1.0 + pre * (1.0 - logistic))
        direct_out[part, :] = back_hidden + back_hidden * turned * gate_slope * gate[...]
    out_msg[...] = packed[...].astype(BF)


def lower_cols_body(
    msg, direct, x_ref, hidden_ref, factor_t, gate, u, v, up2, down1,
    out_msg, back_turned_out,
    wide, packed,
):
    wide[...] = msg[...].astype(F32)
    for oo in range(2):
        part = slice(oo * 256, (oo + 1) * 256)
        passed = (direct[part, :] + unpack_cols(wide, oo)).astype(BF)
        back_hidden = ffn_back(passed, hidden_ref[part, :], u, v, up2, down1)
        pre = x_ref[part, :].astype(F32) * gate[...]
        back_turned = (back_hidden * (pre * sigmoid(pre))).astype(BF)
        back_turned_out[part, :] = back_turned
        pack_cols(dot(factor_t[oo], back_turned), oo, packed)
    out_msg[...] = packed[...].astype(BF)


def channel_grad(outer, inner):
    return jnp.einsum("boc,bic->boi", outer, inner, preferred_element_type=F32).astype(BF)


def on_device(
    inputs,
    cotangent,
    gate_gain,
    key_gain,
    first_factor,
    second_factor,
    up_first,
    up_second,
    down_first,
    down_second_weight,
):
    g = lax.axis_index("segment")
    m = lax.axis_index("mp")
    r = 2 * g + m
    g_arr = g.reshape(1)
    rows = inputs.reshape(8, 256, 256)
    cot_rows = cotangent.reshape(8, 256, 256)
    seq_count = lax.axis_size("seq")
    pairs = [
        (q * 2 + side, (q ^ (seq_count // 2)) * 2 + 1 - side)
        for q in range(seq_count)
        for side in range(2)
    ]

    def swap_mp(value):
        return lax.ppermute(value, ("seq", "mp"), pairs)

    scratch_pack = [(MSG, F32), ((256, 128), F32)]
    (x_msg,) = call(pack_body, "pack_x", [(MSG, BF)], scratch_pack, (g_arr, rows), smem=1)
    (cot_msg,) = call(pack_body, "pack_cot", [(MSG, BF)], scratch_pack, (g_arr, cot_rows), smem=1)
    x_msg = exchange(x_msg, QUARTER_ORDER)
    cot_msg = exchange(cot_msg, QUARTER_ORDER)

    first_mine, second_mine = first_factor[0], second_factor[0]
    first_got = swap(lax.dynamic_slice_in_dim(first_mine, 4 * (1 - g), 4, 0), "segment")
    second_got = swap(lax.dynamic_slice_in_dim(second_mine, 4 * (1 - g) + 2 * m, 2, 0), "segment")
    key_got = swap(key_gain, "segment")

    (mixed_msg,) = call(
        first_rows_body,
        "first_rows",
        [(MSG, BF)],
        scratch_pack,
        (g_arr, rows, first_mine, first_got, pick(g, key_gain, key_got)),
        smem=1,
    )
    mixed_msg = exchange(mixed_msg, QUARTER_ORDER)

    first_own = lax.dynamic_slice_in_dim(first_mine, 2 * r, 2, 0)
    first_oth = lax.dynamic_slice_in_dim(first_got, 2 * m, 2, 0)
    second_own = lax.dynamic_slice_in_dim(second_mine, 2 * r, 2, 0)
    first1 = pick(g, first_oth, first_own)
    first1_t = jnp.swapaxes(first1, 1, 2)
    second0, second1 = pick(g, second_own, second_got), pick(g, second_got, second_own)
    second0_t, second1_t = jnp.swapaxes(second0, 1, 2), jnp.swapaxes(second1, 1, 2)

    narrow = jnp.concatenate([up_first[0], down_second_weight[0], down_first[0]], axis=1)
    wide = up_second[0]

    def every_block(own):
        peer = swap_mp(own)
        whole = pick(m, jnp.concatenate([own, peer]), jnp.concatenate([peer, own]))
        other = swap(whole, "segment")
        return pick(g, whole, other), pick(g, other, whole)

    narrow, up2 = every_block(narrow), every_block(wide)
    down1 = [n[:, 256:] for n in narrow]
    gains = jnp.concatenate([gate_gain, key_gain])
    gains_peer = swap_mp(gains)
    gains_all = pick(
        m,
        jnp.concatenate([gains, gains_peer], axis=1),
        jnp.concatenate([gains_peer, gains], axis=1),
    )
    gains_other = swap(gains_all, "segment")
    layers = (pick(g, gains_all, gains_other), pick(g, gains_other, gains_all))
    gate = [layer[0:1] for layer in layers]
    key = [layer[1:2] for layer in layers]
    dense = [
        call(
            prepare_body,
            f"prepare_{layer}",
            [((512, 512), BF)] * 2,
            [],
            (narrow[layer][:, :128], narrow[layer][:, 128:256]),
        )
        for layer in range(2)
    ]

    act = ((512, 512), BF)
    next_msg, mixed0, x0, hidden0, turned0, middle = call(
        forward_cols_body,
        "forward_cols",
        [(MSG, BF)] + [act] * 5,
        [(MSG, F32)] * 2,
        (mixed_msg, x_msg, second0, gate[0], key[1], *dense[0], up2[0], down1[0]),
    )
    msg = exchange(next_msg, ROWS_ORDER)

    scratch_rows = [(MSG, F32), (MSG, F32), ((256, 128), F32), ((4, 256, 128), F32)]
    out_rows = [(MSG, BF), ((2, 256, 512), BF)]
    next_msg, scaled1 = call(
        rows_body, "rows_1", out_rows, scratch_rows, (msg, first1, jnp.ones((1, 512), F32))
    )
    msg = exchange(next_msg, ROWS_ORDER)

    next_msg, mixed1, back_turned1, direct = call(
        upper_cols_body,
        "upper_cols",
        [(MSG, BF), act, act, ((512, 512), F32)],
        [(MSG, F32)] * 3,
        (msg, cot_msg, middle, second1, second1_t, gate[1], *dense[1], up2[1], down1[1]),
    )
    msg = exchange(next_msg, ROWS_ORDER)
    cols = (2, 256, 512)
    second_grad1 = channel_grad(back_turned1.reshape(cols), mixed1.reshape(cols))

    next_msg, back_rows1 = call(rows_body, "rows_1_back", out_rows, scratch_rows, (msg, first1_t, key[1]))
    msg = exchange(next_msg, ROWS_ORDER)
    first_grad1 = channel_grad(back_rows1, scaled1)

    next_msg, back_turned0 = call(
        lower_cols_body,
        "lower_cols",
        [(MSG, BF), act],
        [(MSG, F32)] * 2,
        (msg, direct, x0, hidden0, second0_t, gate[0], *dense[0], up2[0], down1[0]),
    )
    msg = exchange(next_msg, ROWS_ORDER)
    second_grad0 = channel_grad(back_turned0.reshape(cols), mixed0.reshape(cols))

    own = lax.dynamic_slice_in_dim(rows, 2 * r, 2, 0)
    peer = swap(lax.dynamic_slice_in_dim(rows, 2 * (2 * g + 1 - m), 2, 0), "mp")
    x_rows = pick(m, jnp.concatenate([own, peer], axis=2), jnp.concatenate([peer, own], axis=2))
    (first_grad0,) = call(
        last_rows_body,
        "last_rows",
        [((2, 256, 256), BF)],
        [(MSG, F32), ((4, 256, 128), F32)],
        (msg, x_rows, key[0]),
    )

    def gather_mp(grad):
        halves = grad.reshape(2, 2, 128, 256)
        mine = lax.dynamic_index_in_dim(halves, m, 1, False)
        theirs = swap(lax.dynamic_index_in_dim(halves, 1 - m, 1, False), "mp")
        return pick(m, jnp.concatenate([mine, theirs]), jnp.concatenate([theirs, mine]))

    def place(grad0, grad1):
        four0, four1 = gather_mp(grad0), gather_mp(grad1)
        from1 = lax.ppermute(four1, "segment", [(0, 1)])
        from0 = lax.ppermute(four0, "segment", [(1, 0)])
        mine = pick(g, four0, four1)
        theirs = pick(g, from0, from1)
        eight = pick(g, jnp.concatenate([mine, theirs]), jnp.concatenate([theirs, mine]))
        return eight.astype(F32)[None]

    return place(first_grad0, first_grad1), place(second_grad0, second_grad1)


def solution(mesh):
    placed = (
        P("seq", "mp"),
        P("seq", "mp"),
        P("segment", "mp"),
        P("segment", "mp"),
        P("segment", "seq", None, None),
        P("segment", "seq", None, None),
        P("segment", "mp", None, None),
        P("segment", "mp", None, None),
        P("segment", "mp", None, None),
        P("segment", "mp", None, None),
    )
    return jax.shard_map(
        on_device,
        mesh=mesh,
        in_specs=placed,
        out_specs=(P("segment", "seq", "mp", None), P("segment", "seq", "mp", None)),
        check_vma=False,
    )
```

```python
import math

import jax
import jax.numpy as jnp
from jax import lax
from jax.experimental import pallas as pl
from jax.experimental.pallas import tpu as pltpu
from jax.sharding import PartitionSpec as P


ROWS_ORDER = ("seq", "segment", "mp")
QUARTER_ORDER = ("mp", "seq", "segment")
BF = jnp.bfloat16
F32 = jnp.float32
MSG = (2048, 128)
OWNERS = 128
TILES = (OWNERS, 16, 128)
PAIR = (OWNERS, 2, 16, 128)
VMEM_BYTES = 67043328
SPARE = 2**17
WEIGHT_ROWS = 2560


def exchange(message, order):
    return lax.all_to_all(message, order, split_axis=0, concat_axis=0, tiled=True)


def swap(value, axis):
    return lax.ppermute(value, axis, [(0, 1), (1, 0)])


def dot(a, b):
    return jnp.dot(a, b, preferred_element_type=F32)


def dot_nt(a, b):
    return lax.dot_general(a, b, (((1,), (1,)), ((), ())), preferred_element_type=F32)


def sigmoid(v):
    return 0.5 * jnp.tanh(0.5 * v) + 0.5


def slope(v):
    s = sigmoid(v)
    return s * (1.0 + v * (1.0 - s))


class Loaded:
    def __init__(self, source, buffer, sem):
        self.copy, self.buffer, self.ready = pltpu.make_async_copy(source, buffer, sem), buffer, False
        self.copy.start()

    def get(self):
        if not self.ready:
            self.copy.wait()
            self.ready = True
        return self.buffer

    def __getitem__(self, index):
        return self.get()[index]


class Result:
    def __init__(self, target, buffer, sems):
        self.target, self.ref, self.sems, self.copies = target, buffer, sems, []

    def send(self, *index):
        source, target = (self.ref.at[index], self.target.at[index]) if index else (self.ref, self.target)
        copy = pltpu.make_async_copy(source, target, self.sems.at[len(self.copies)])
        copy.start()
        self.copies.append(copy)


class Near:
    def __init__(self, value):
        self.value = value


def call(body, outs, scratch, args, after=()):
    near_in = [isinstance(a, Near) for a in args]
    near_out = [isinstance(o, Near) for o in outs]
    args = [a.value if isinstance(a, Near) else a for a in args]
    args = [a if isinstance(a, tuple) else (a, None, a.shape) for a in args]
    outs = [o.value if isinstance(o, Near) else o for o in outs]
    far_in = [n for n, near in enumerate(near_in) if not near]
    far_out = [n for n, near in enumerate(near_out) if not near]
    total = len(args) + len(after)

    def kernel(*refs):
        sources, targets = refs[: len(args)], refs[total : total + len(outs)]
        rest = refs[total + len(outs) :]
        buffers, rest = rest[: len(far_in)], rest[len(far_in) :]
        results, rest = rest[: len(far_out)], rest[len(far_out) :]
        sems, out_sems, *extra = rest
        loads, stores = list(sources), list(targets)
        for k, n in enumerate(far_in):
            view = args[n][1]
            loads[n] = Loaded(view(sources[n]) if view else sources[n], buffers[k], sems.at[k])
        for k, n in enumerate(far_out):
            stores[n] = Result(targets[n], results[k], out_sems.at[k])
        body(loads, stores, *extra)
        for n in far_in:
            loads[n].get()
        for n in far_out:
            if not stores[n].copies:
                stores[n].send()
        for n in far_out:
            for copy in stores[n].copies:
                copy.wait()

    moved = sum(math.prod(shape) * a.dtype.itemsize for a, view, shape in args)
    moved += sum(math.prod(shape) * jnp.dtype(dtype).itemsize for shape, dtype in outs)
    held = sum(math.prod(args[n][0].shape) * args[n][0].dtype.itemsize for n in range(len(args)) if near_in[n])
    held += sum(math.prod(outs[n][0]) * jnp.dtype(outs[n][1]).itemsize for n in range(len(outs)) if near_out[n])
    near, far = pl.BlockSpec(memory_space=pltpu.VMEM), pl.BlockSpec(memory_space=pltpu.HBM)
    return pl.pallas_call(
        kernel,
        out_shape=tuple(jax.ShapeDtypeStruct(*o) for o in outs),
        in_specs=[near if n else far for n in near_in]
        + [pl.BlockSpec(memory_space=pl.ANY)] * len(after),
        out_specs=tuple(near if n else far for n in near_out),
        scratch_shapes=[pltpu.VMEM(args[n][2], args[n][0].dtype) for n in far_in]
        + [pltpu.VMEM(*outs[n]) for n in far_out]
        + [pltpu.SemaphoreType.DMA((max(1, len(far_in)),)), pltpu.SemaphoreType.DMA((max(1, len(far_out)), 8))]
        + [pltpu.VMEM(s, d) for s, d in scratch],
        compiler_params=pltpu.CompilerParams(vmem_limit_bytes=VMEM_BYTES - held - SPARE),
        cost_estimate=pl.CostEstimate(flops=10**8, bytes_accessed=moved, transcendentals=0),
    )(*[a[0] for a in args], *after)


def core():
    return lax.axis_index("segment")


def side():
    return lax.axis_index("mp")


def widen(msg, wide):
    wide[...] = msg.reshape(MSG).astype(F32)


def narrow(packed):
    return packed[...].reshape(TILES).astype(BF)


def pack_quarter(values, a, out, temp):
    for h in range(2):
        temp[...] = values[:, h * 128 : (h + 1) * 128]
        for mm in range(2):
            for oo in range(2):
                row = mm * 1024 + a * 4 + oo * 2 + h
                out[pl.ds(row, 64, stride=16), :] = temp[pl.ds(mm * 2 + oo, 64, stride=4), :]


def unpack_quarter(source, oo):
    parts = [
        source[pl.ds(mm * 1024 + oo * 2 + h, 256, stride=4), :] for mm in range(2) for h in range(2)
    ]
    return jnp.concatenate(parts, axis=1)


def pack_quarter_rows(values, a, out, temp):
    for h in range(2):
        temp[...] = values[:, h * 128 : (h + 1) * 128]
        for oo in range(2):
            out[pl.ds(a * 4 + oo * 2 + h, 128, stride=16), :] = temp[pl.ds(oo, 128, stride=2), :]


def unpack_quarter_rows(source, oo, temp):
    for mm in range(2):
        for h in range(2):
            for a in range(4):
                temp[mm * 2 + h, pl.ds(a, 64, stride=4), :] = source[
                    pl.ds(mm * 16 + a * 4 + oo * 2 + h, 64, stride=32), :
                ]
    return jnp.concatenate([temp[n] for n in range(4)], axis=1)


def pack_cols(values, oo, out):
    for cq in range(4):
        out[pl.ds(oo * 4 + cq, 256, stride=8), :] = values[:, cq * 128 : (cq + 1) * 128]


def unpack_cols(source, oo):
    return jnp.concatenate(
        [source[pl.ds(oo * 4 + cq, 256, stride=8), :] for cq in range(4)], axis=1
    )


def pack_rows(values, a2, out, temp):
    for cq in range(4):
        temp[...] = values[:, cq * 128 : (cq + 1) * 128]
        for oo in range(2):
            out[pl.ds(a2 * 8 + oo * 4 + cq, 128, stride=16), :] = temp[pl.ds(oo, 128, stride=2), :]


def unpack_rows(source, a2, temp):
    for cq in range(4):
        for oo in range(2):
            temp[cq, pl.ds(oo, 128, stride=2), :] = source[
                pl.ds(a2 * 8 + oo * 4 + cq, 128, stride=16), :
            ]
    return jnp.concatenate([temp[cq] for cq in range(4)], axis=1)


def slice_body(ins, outs):
    outs[0].ref[...] = ins[0][...]


def pack_cot_body(ins, outs, packed, temp):
    (x_ref,) = ins
    for a in range(4):
        pack_quarter_rows(x_ref[a].astype(F32), a, packed, temp)
    outs[0][...] = narrow(packed)


def pack_body(ins, outs, packed, temp):
    x_ref, up1, ds, d1, up2 = ins
    out, x_out, x_tiles = outs
    for i in range(2):
        out[i * 128 : (i + 1) * 128, :] = up1[i]
        out[256 + i * 128 : 256 + (i + 1) * 128, :] = ds[i]
        out[512 + i * 512 : 512 + (i + 1) * 512, :] = d1[i]
        for cq in range(4):
            row = 1536 + (i * 4 + cq) * 128
            out[row : row + 128, :] = up2[i, :, cq * 128 : (cq + 1) * 128]
    for a in range(4):
        x_out[a] = x_ref[a]
        pack_quarter(x_ref[a].astype(F32), a, packed, temp)
    x_tiles[...] = narrow(packed)


def first_rows_body(ins, outs, packed, temp):
    x_ref, x_tiles, key_mine, key_got, mine_ref, got_ref = ins
    g = core()
    key = jnp.where(g == 0, key_mine[...], key_got[...])
    for a in range(4):
        factor = jnp.where(g == 0, mine_ref[a], got_ref[4 * g + a])
        scaled = (x_ref[a].astype(F32) * key).astype(BF)
        pack_quarter(dot(factor, scaled), a, packed, temp)
    outs[0][:, 1] = x_tiles[...]
    outs[0][:, 0] = narrow(packed)


def weights_body(layer, ins, outs):
    g, m = core(), side()
    own_ref, peer_ref, other_ref, both_ref = ins[:4]
    u_ref, v_ref, up2_ref, d1_ref = (o.ref for o in outs[:4])

    def block(start, rows, mine):
        part = slice(start, start + rows)
        here = jnp.where(mine, own_ref[part, :], peer_ref[part, :])
        there = jnp.where(mine, other_ref[part, :], both_ref[part, :])
        return jnp.where(g == layer, here, there)

    rho = lax.broadcasted_iota(jnp.int32, (128, 512), 0)
    gam = lax.broadcasted_iota(jnp.int32, (128, 512), 1)
    same = (gam // 128) * 32 + gam % 32 == rho
    for k in range(4):
        i, mine = k % 2, m == k // 2
        spot = jnp.where(same & ((gam // 32) % 4 == k), 1.0, 0.0).astype(BF)
        u_ref[k * 128 : (k + 1) * 128, :] = dot(block(i * 128, 128, mine), spot).astype(BF)
        spread = lax.dot_general(
            spot, block(256 + i * 128, 128, mine), (((0,), (0,)), ((), ())),
            preferred_element_type=F32,
        )
        v_ref[:, k * 128 : (k + 1) * 128] = spread.astype(BF)
        d1_ref[k] = block(512 + i * 512, 512, mine)
        for cq in range(4):
            up2_ref[k, :, cq * 128 : (cq + 1) * 128] = block(1536 + (i * 4 + cq) * 128, 128, mine)
        for out in outs[2:4]:
            out.send(k)
    if layer == 1:
        return
    own, peer, other, both = (n[...] for n in ins[6:10])
    for half in range(2):
        lanes = slice(half * 256, (half + 1) * 256)
        mine = jnp.where(m == half, own, peer)
        got = jnp.where(m == half, other, both)
        outs[4].ref[:, lanes] = jnp.where(g == 0, mine, got)
        outs[5].ref[:, lanes] = jnp.where(g == 0, got, mine)
    for oo in range(2):
        outs[6].ref[oo] = jnp.where(g == 0, ins[4][oo], ins[5][oo])


def factors_body(ins, outs):
    g = core()
    first_mine, first_got, second_mine, second_got = ins
    first1, first1_t, second1, second1_t, second0_t = (o.ref for o in outs)
    for i in range(2):
        first = jnp.where(g == 1, first_mine[i], first_got[i])
        first1[i] = first
        first1_t[i] = first.astype(F32).T.astype(BF)
        second = jnp.where(g == 1, second_mine[i], second_got[i])
        second1[i] = second
        second1_t[i] = second.astype(F32).T.astype(BF)
        second = jnp.where(g == 0, second_mine[i], second_got[i])
        second0_t[i] = second.astype(F32).T.astype(BF)


def forward_cols_body(ins, outs, wide, wide_x, packed):
    msg, factor, gains0, gains1, u, up2, down1, v = ins
    out_msg, mixed_out, x_out, hidden_out, middle_out = outs
    widen(msg[:, 0], wide)
    widen(msg[:, 1], wide_x)
    for oo in range(2):
        mixed = unpack_quarter(wide, oo).astype(BF)
        x = unpack_quarter(wide_x, oo)
        turned = dot(factor[oo], mixed).astype(BF)
        pre = x * gains0[0:1, :]
        hidden = (x + pre * sigmoid(pre) * turned.astype(F32)).astype(BF)
        for out, value in ((mixed_out, mixed), (x_out, x.astype(BF)), (hidden_out, hidden)):
            out.ref[oo] = value
            out.send(oo)
        permuted = dot(hidden, u[...]).astype(BF)
        folds = []
        for j in range(4):
            preact = dot(permuted[:, j * 128 : (j + 1) * 128], up2[j])
            active = (preact * sigmoid(preact)).astype(BF)
            folds.append(dot(active, down1[j]).astype(BF))
        out = dot(jnp.concatenate(folds, axis=1), v[...])
        middle = (hidden.astype(F32) + out).astype(BF)
        middle_out.ref[oo] = middle
        middle_out.send(oo)
        pack_cols(middle.astype(F32) * gains1[1:2, :], oo, packed)
    out_msg[...] = narrow(packed)


def rows_body(ins, outs, wide, packed, temp, temp4):
    msg, factor, more = ins
    widen(msg[...], wide)
    for a2 in range(2):
        values = unpack_rows(wide, a2, temp4).astype(BF)
        outs[1].ref[a2] = values
        outs[1].send(a2)
        result = dot(factor[a2], values)
        if len(outs[0].shape) == 3:
            result = result * more[1:2, :]
        pack_rows(result, a2, packed, temp)
    if len(outs[0].shape) == 3:
        outs[0][...] = narrow(packed)
    else:
        outs[0][:, 1] = more[...]
        outs[0][:, 0] = narrow(packed)


def grad_body(ins, outs):
    outer, inner = ins
    for i in range(2):
        grad = dot_nt(outer[i], inner[i]).astype(BF)
        outs[0].ref[0, i] = grad[:128]
        outs[0].ref[1, i] = grad[128:]


def second_grads_body(ins, outs, own, other):
    g, m = core(), side()
    outer, inner, upper = ins
    for i in range(2):
        grad = dot_nt(outer[i], inner[i]).astype(BF)
        for half in range(2):
            lower = grad[half * 128 : (half + 1) * 128]
            own[half, i] = jnp.where(g == 0, lower, upper[half, i])
            other[half, i] = jnp.where(g == 0, upper[half, i], lower)
    for out, (source, half) in zip(outs, ((own, m), (own, 1 - m), (other, m), (other, 1 - m))):
        out[...] = source[half]


def last_rows_body(ins, outs, wide, temp4):
    msg, x_own, x_peer, gains, upper = ins
    m = side()
    widen(msg[...], wide)
    for a2 in range(2):
        values = unpack_rows(wide, a2, temp4).astype(BF)
        own, peer = x_own[a2].astype(F32), x_peer[a2].astype(F32)
        low = (jnp.where(m == 0, own, peer) * gains[1:2, :256]).astype(BF)
        high = (jnp.where(m == 0, peer, own) * gains[1:2, 256:]).astype(BF)
        grad = dot_nt(values[:, :256], low) + dot_nt(values[:, 256:], high)
        outs[0][0, a2] = grad[:128].astype(BF)
        outs[0][1, a2] = grad[128:].astype(BF)
    for half in range(2):
        outs[0][2 + half] = upper[half]


def collect_body(ins, outs):
    g, m = core(), side()
    owners = 2 * g + m, 2 * (1 - g) + m, 2 * g + 1 - m, 2 * (1 - g) + 1 - m
    for n, owner in enumerate(owners):
        part = pl.ds(2 * owner, 2)
        outs[0].ref[part] = ins[n][...].astype(F32)
        outs[0].send(part)


def ffn_back(cot, hidden, u, v, up2, down1):
    permuted = dot(hidden, u[...]).astype(BF)
    fold = dot_nt(cot, v[...]).astype(BF)
    perms = []
    for j in range(4):
        block = slice(j * 128, (j + 1) * 128)
        preact = dot(permuted[:, block], up2[j])
        back_active = dot_nt(fold[:, block], down1[j])
        back_preact = (back_active * slope(preact)).astype(BF)
        perms.append(dot_nt(back_preact, up2[j]).astype(BF))
    return cot.astype(F32) + dot_nt(jnp.concatenate(perms, axis=1), u[...])


def upper_cols_body(ins, outs, wide, wide_c, packed, temp4):
    msg, factor, x_ref, gains, v, u, up2, down1, factor_t = ins
    out_msg, mixed_out, back_turned_out, direct_out = outs
    widen(msg[:, 0], wide)
    widen(msg[:, 1], wide_c)
    for oo in range(2):
        mixed = unpack_cols(wide, oo).astype(BF)
        cot = unpack_quarter_rows(wide_c, oo, temp4).astype(BF)
        mixed_out.ref[oo] = mixed
        mixed_out.send(oo)
        gate = gains[0:1, :]
        x = x_ref[oo].astype(F32)
        turned = dot(factor[oo], mixed).astype(BF).astype(F32)
        pre = x * gate
        logistic = sigmoid(pre)
        gated = pre * logistic
        hidden = (x + gated * turned).astype(BF)
        back_hidden = ffn_back(cot, hidden, u, v, up2, down1)
        back_turned = (back_hidden * gated).astype(BF)
        back_turned_out.ref[oo] = back_turned
        back_turned_out.send(oo)
        pack_cols(dot(factor_t[oo], back_turned), oo, packed)
        gate_slope = logistic * (1.0 + pre * (1.0 - logistic))
        direct_out.ref[oo] = back_hidden + back_hidden * turned * gate_slope * gate
        direct_out.send(oo)
    out_msg[...] = narrow(packed)


def lower_cols_body(ins, outs, wide, packed):
    msg, direct0, hidden_ref, v, u, up2, down1, direct1, x_ref, gains, factor_t = ins
    direct = direct0, direct1
    out_msg, back_turned_out = outs
    widen(msg[...], wide)
    for oo in range(2):
        passed = (direct[oo][...] + unpack_cols(wide, oo)).astype(BF)
        back_hidden = ffn_back(passed, hidden_ref[oo], u, v, up2, down1)
        pre = x_ref[oo].astype(F32) * gains[0:1, :]
        back_turned = (back_hidden * (pre * sigmoid(pre))).astype(BF)
        back_turned_out.ref[oo] = back_turned
        back_turned_out.send(oo)
        pack_cols(dot(factor_t[oo], back_turned), oo, packed)
    out_msg[...] = narrow(packed)


def layer_pair(
    inputs,
    cotangent,
    gate_gain,
    key_gain,
    first_factor,
    second_factor,
    up_first,
    up_second,
    down_first,
    down_second_weight,
):
    g, m = core(), side()
    rows = inputs.reshape(8, 256, 256)
    cot_rows = cotangent.reshape(8, 256, 256)
    first_mine, second_mine = first_factor[0], second_factor[0]
    seq_count = lax.axis_size("seq")

    def swap_z(value, layers):
        pairs = [
            ((layer * seq_count + q) * 2 + end, (layer * seq_count + (q ^ (seq_count // 2))) * 2 + 1 - end)
            for layer in layers
            for q in range(seq_count)
            for end in range(2)
        ]
        return lax.ppermute(value, ("segment", "seq", "mp"), pairs)

    def give(value, layer):
        return lax.ppermute(value, "segment", [(layer, 1 - layer)])

    def two(array):
        def view(ref):
            return ref.at[pl.ds(2 * (2 * core() + side()), 2)]

        return array, view, (2,) + array.shape[1:]

    def four(array):
        def view(ref):
            return ref.at[pl.ds(4 * core(), 4)]

        return array, view, (4,) + array.shape[1:]

    def part(array, n):
        return array, lambda ref: ref.at[n], array.shape[1:]

    tiles = Near((TILES, BF))
    scratch_pack = [(MSG, F32), ((256, 128), F32)]

    key_got = swap(key_gain, "segment")
    own, x_rows, x_tiles = call(
        pack_body,
        [Near(((WEIGHT_ROWS, 128), BF)), Near(((4, 256, 256), BF)), tiles],
        scratch_pack,
        (four(rows), up_first[0], down_second_weight[0], down_first[0], up_second[0]),
    )
    first_got = swap(first_mine, "segment")
    peer0 = swap_z(own, (0,))
    (rows_msg,) = call(
        first_rows_body,
        [Near((PAIR, BF))],
        scratch_pack,
        (Near(x_rows), Near(x_tiles), key_gain, key_got, Near(first_mine), Near(first_got)),
    )

    def send(message, order=ROWS_ORDER):
        shape = message.shape
        return exchange(message.reshape(-1, 128), order).reshape(shape)

    msg = send(rows_msg, QUARTER_ORDER)

    second_got = swap(second_mine, "segment")
    gains = jnp.concatenate([gate_gain, key_gain])
    gains_peer = swap_z(gains, (0, 1))
    gains_got = swap(gains, "segment")
    gains_both = swap(gains_peer, "segment")
    other0 = give(own, 0)
    both0 = give(peer0, 0)
    square = ((512, 512), BF)
    layer_outs = [square, square, ((4, 128, 512), BF), ((4, 512, 128), BF)]
    gain = ((2, 512), F32)
    pair = ((2, 256, 256), BF)
    u0, v0, up0, down0, gains0, gains1, second0 = call(
        lambda ins, outs: weights_body(0, ins, outs),
        layer_outs + [gain, gain, pair],
        [],
        (
            own, peer0, other0, both0, two(second_mine), two(second_got),
            gains, gains_peer, gains_got, gains_both,
        ),
    )

    (x_sent,) = call(
        slice_body,
        [((2, 256, 256), BF)],
        [],
        ((rows, lambda ref: ref.at[pl.ds(2 * (2 * core() + 1 - side()), 2)], (2, 256, 256)),),
        after=(u0,),
    )
    x_peer = swap(x_sent, "mp")

    block = ((2, 256, 512), BF)
    next_msg, mixed0, x0, hidden0, middle = call(
        forward_cols_body,
        [tiles] + [block] * 4,
        [(MSG, F32)] * 3,
        (Near(msg), second0, gains0, gains1, u0, up0, down0, v0),
    )
    msg = send(next_msg)
    peer1 = swap_z(own, (1,))
    other1 = give(own, 1)
    first1, first1_t, second1, second1_t, second0_t = call(
        factors_body,
        [pair] * 5,
        [],
        (two(first_mine), two(first_got), two(second_mine), two(second_got)),
        after=(next_msg,),
    )
    (cot_tiles,) = call(pack_cot_body, [tiles], scratch_pack, (four(cot_rows),), after=(first1,))

    scratch_rows = [(MSG, F32), (MSG, F32), ((256, 128), F32), ((4, 256, 128), F32)]
    next_msg, scaled1 = call(
        rows_body, [Near((PAIR, BF)), block], scratch_rows, (Near(msg), first1, Near(cot_tiles))
    )
    msg = send(next_msg)
    both1 = give(peer1, 1)
    u1, v1, up1, down1 = call(
        lambda ins, outs: weights_body(1, ins, outs), layer_outs, [], (own, peer1, other1, both1)
    )
    next_msg, mixed1, back_turned1, direct = call(
        upper_cols_body,
        [tiles, block, block, ((2, 256, 512), F32)],
        [(MSG, F32)] * 3 + [((4, 256, 128), F32)],
        (Near(msg), *(Near(a) for a in (second1, middle, gains1, v1, u1, up1, down1, second1_t))),
    )
    msg = send(next_msg)

    halves = ((2, 2, 128, 256), BF)

    def channel_grad(outer, inner, after):
        (grad,) = call(grad_body, [halves], [], (outer, inner), after=(after,))
        return grad

    second_grad1 = channel_grad(back_turned1, mixed1, next_msg)

    next_msg, back_rows1 = call(
        rows_body, [tiles, block], scratch_rows, (Near(msg), first1_t, gains1)
    )
    msg = send(next_msg)
    first_grad1 = channel_grad(back_rows1, scaled1, next_msg)

    next_msg, back_turned0 = call(
        lower_cols_body,
        [tiles, block],
        [(MSG, F32)] * 2,
        (Near(msg), part(direct, 0), hidden0, v0, u0, up0, down0, part(direct, 1), x0, gains0, second0_t),
    )
    msg = send(next_msg)
    half = Near(((2, 128, 256), BF))
    mine, own_theirs, other_mine, other_theirs = call(
        second_grads_body,
        [half] * 4,
        [halves] * 2,
        (back_turned0, mixed0, second_grad1),
        after=(next_msg,),
    )
    from_side = swap(own_theirs, "mp")
    from_both = lax.ppermute(other_theirs, ("segment", "mp"), [(0, 3), (1, 2), (2, 1), (3, 0)])
    from_core = swap(other_mine, "segment")

    (message,) = call(
        last_rows_body,
        [Near(((4, 2, 128, 256), BF))],
        [(MSG, F32), ((4, 256, 128), F32)],
        (Near(msg), two(rows), x_peer, gains0, first_grad1),
    )
    grad_first = lax.all_to_all(message, ("segment", "mp"), split_axis=0, concat_axis=0, tiled=True)
    (grad_second,) = call(
        collect_body,
        [((8, 128, 256), F32)],
        [],
        (mine, from_core, from_side, from_both),
        after=(message,),
    )
    return grad_first.reshape(1, 8, 128, 256).astype(F32), grad_second[None]


def solution(mesh):
    placed = (
        P("seq", "mp"),
        P("seq", "mp"),
        P("segment", "mp"),
        P("segment", "mp"),
        P("segment", "seq", None, None),
        P("segment", "seq", None, None),
        P("segment", "mp", None, None),
        P("segment", "mp", None, None),
        P("segment", "mp", None, None),
        P("segment", "mp", None, None),
    )
    return jax.shard_map(
        layer_pair,
        mesh=mesh,
        in_specs=placed,
        out_specs=(P("segment", "seq", "mp", None), P("segment", "seq", "mp", None)),
        check_vma=False,
    )
```

```python
import math

import jax
import jax.numpy as jnp
from jax import lax
from jax.experimental import pallas as pl
from jax.experimental.pallas import tpu as pltpu
from jax.sharding import PartitionSpec as P


ROWS_ORDER = ("seq", "segment", "mp")
QUARTER_ORDER = ("mp", "seq", "segment")
BF = jnp.bfloat16
F32 = jnp.float32
MSG = (2048, 128)
OWNERS = 128
PAIR = (4096, 128)
VMEM_BYTES = 67043328
SPARE = 16 * 2**20
WEIGHT_ROWS = 2560


def exchange(message, order):
    return lax.all_to_all(message, order, split_axis=0, concat_axis=0, tiled=True)


def swap(value, axis):
    return lax.ppermute(value, axis, [(0, 1), (1, 0)])


def dot(a, b):
    return jnp.dot(a, b, preferred_element_type=F32)


def dot_nt(a, b):
    return lax.dot_general(a, b, (((1,), (1,)), ((), ())), preferred_element_type=F32)


def sigmoid(v):
    return 0.5 * jnp.tanh(0.5 * v) + 0.5


def slope(v):
    s = sigmoid(v)
    return s * (1.0 + v * (1.0 - s))


class Loaded:
    def __init__(self, source, buffer, sem):
        self.copy, self.buffer, self.ready = pltpu.make_async_copy(source, buffer, sem), buffer, False
        self.copy.start()

    def get(self):
        if not self.ready:
            self.copy.wait()
            self.ready = True
        return self.buffer

    def __getitem__(self, index):
        return self.get()[index]


class Result:
    def __init__(self, target, buffer, sems):
        self.target, self.ref, self.sems, self.copies = target, buffer, sems, []

    def send(self, *index):
        source, target = (self.ref.at[index], self.target.at[index]) if index else (self.ref, self.target)
        copy = pltpu.make_async_copy(source, target, self.sems.at[len(self.copies)])
        copy.start()
        self.copies.append(copy)


class Near:
    def __init__(self, value):
        self.value = value


def call(body, outs, scratch, args, after=()):
    near_in = [isinstance(a, Near) for a in args]
    near_out = [isinstance(o, Near) for o in outs]
    args = [a.value if isinstance(a, Near) else a for a in args]
    args = [a if isinstance(a, tuple) else (a, None, a.shape) for a in args]
    outs = [o.value if isinstance(o, Near) else o for o in outs]
    far_in = [n for n, near in enumerate(near_in) if not near]
    far_out = [n for n, near in enumerate(near_out) if not near]
    total = len(args) + len(after)

    def kernel(*refs):
        sources, targets = refs[: len(args)], refs[total : total + len(outs)]
        rest = refs[total + len(outs) :]
        buffers, rest = rest[: len(far_in)], rest[len(far_in) :]
        results, rest = rest[: len(far_out)], rest[len(far_out) :]
        sems, out_sems, *extra = rest
        loads, stores = list(sources), list(targets)
        for k, n in enumerate(far_in):
            view = args[n][1]
            loads[n] = Loaded(view(sources[n]) if view else sources[n], buffers[k], sems.at[k])
        for k, n in enumerate(far_out):
            stores[n] = Result(targets[n], results[k], out_sems.at[k])
        body(loads, stores, *extra)
        for n in far_in:
            loads[n].get()
        for n in far_out:
            if not stores[n].copies:
                stores[n].send()
        for n in far_out:
            for copy in stores[n].copies:
                copy.wait()

    moved = sum(math.prod(shape) * a.dtype.itemsize for a, view, shape in args)
    moved += sum(math.prod(shape) * jnp.dtype(dtype).itemsize for shape, dtype in outs)
    held = sum(math.prod(args[n][0].shape) * args[n][0].dtype.itemsize for n in range(len(args)) if near_in[n])
    held += sum(math.prod(outs[n][0]) * jnp.dtype(outs[n][1]).itemsize for n in range(len(outs)) if near_out[n])
    near, far = pl.BlockSpec(memory_space=pltpu.VMEM), pl.BlockSpec(memory_space=pltpu.HBM)
    return pl.pallas_call(
        kernel,
        out_shape=tuple(
            jax.ShapeDtypeStruct(*o) if n else pltpu.HBM(*o) for n, o in zip(near_out, outs)
        ),
        in_specs=[near if n else far for n in near_in]
        + [pl.BlockSpec(memory_space=pl.ANY)] * len(after),
        out_specs=tuple(near if n else far for n in near_out),
        scratch_shapes=[pltpu.VMEM(args[n][2], args[n][0].dtype) for n in far_in]
        + [pltpu.VMEM(*outs[n]) for n in far_out]
        + [pltpu.SemaphoreType.DMA((max(1, len(far_in)),)), pltpu.SemaphoreType.DMA((max(1, len(far_out)), 8))]
        + [pltpu.VMEM(s, d) for s, d in scratch],
        compiler_params=pltpu.CompilerParams(vmem_limit_bytes=VMEM_BYTES - held - SPARE),
        cost_estimate=pl.CostEstimate(flops=10**8, bytes_accessed=moved, transcendentals=0),
    )(
        *[a[0] if n else pltpu.with_memory_space_constraint(a[0], pltpu.HBM) for n, a in zip(near_in, args)],
        *after,
    )


def core():
    return lax.axis_index("segment")


def side():
    return lax.axis_index("mp")


def widen(msg, wide):
    wide[...] = msg[...].astype(F32)


def narrow(packed):
    return packed[...].astype(BF)


def joined(packed, tiles):
    parts = [values.reshape(OWNERS, 16, 128) for values in (packed[...], tiles[...].astype(F32))]
    return jnp.concatenate(parts, axis=1).reshape(PAIR).astype(BF)


def parted(msg, wide, wide_more):
    both = msg[...].astype(F32).reshape(OWNERS, 32, 128)
    wide[...] = both[:, :16].reshape(MSG)
    wide_more[...] = both[:, 16:].reshape(MSG)


def pack_quarter(values, a, out, temp):
    for h in range(2):
        temp[...] = values[:, h * 128 : (h + 1) * 128]
        for mm in range(2):
            for oo in range(2):
                row = mm * 1024 + a * 4 + oo * 2 + h
                out[pl.ds(row, 64, stride=16), :] = temp[pl.ds(mm * 2 + oo, 64, stride=4), :]


def unpack_quarter(source, oo):
    parts = [
        source[pl.ds(mm * 1024 + oo * 2 + h, 256, stride=4), :] for mm in range(2) for h in range(2)
    ]
    return jnp.concatenate(parts, axis=1)


def pack_quarter_rows(values, a, out, temp):
    for h in range(2):
        temp[...] = values[:, h * 128 : (h + 1) * 128]
        for oo in range(2):
            out[pl.ds(a * 4 + oo * 2 + h, 128, stride=16), :] = temp[pl.ds(oo, 128, stride=2), :]


def unpack_quarter_rows(source, oo, temp):
    for mm in range(2):
        for h in range(2):
            for a in range(4):
                temp[mm * 2 + h, pl.ds(a, 64, stride=4), :] = source[
                    pl.ds(mm * 16 + a * 4 + oo * 2 + h, 64, stride=32), :
                ]
    return jnp.concatenate([temp[n] for n in range(4)], axis=1)


def pack_cols(values, oo, out):
    for cq in range(4):
        out[pl.ds(oo * 4 + cq, 256, stride=8), :] = values[:, cq * 128 : (cq + 1) * 128]


def unpack_cols(source, oo):
    return jnp.concatenate(
        [source[pl.ds(oo * 4 + cq, 256, stride=8), :] for cq in range(4)], axis=1
    )


def pack_rows(values, a2, out, temp):
    for cq in range(4):
        temp[...] = values[:, cq * 128 : (cq + 1) * 128]
        for oo in range(2):
            out[pl.ds(a2 * 8 + oo * 4 + cq, 128, stride=16), :] = temp[pl.ds(oo, 128, stride=2), :]


def unpack_rows(source, a2, temp):
    for cq in range(4):
        for oo in range(2):
            temp[cq, pl.ds(oo, 128, stride=2), :] = source[
                pl.ds(a2 * 8 + oo * 4 + cq, 128, stride=16), :
            ]
    return jnp.concatenate([temp[cq] for cq in range(4)], axis=1)


def slice_body(ins, outs):
    outs[0].ref[...] = ins[0][...]


def pack_cot_body(ins, outs, packed, temp):
    (x_ref,) = ins
    for a in range(4):
        pack_quarter_rows(x_ref[a].astype(F32), a, packed, temp)
    outs[0][...] = narrow(packed)


def pack_body(ins, outs, packed, temp):
    x_ref, up1, ds, d1, up2 = ins
    out, x_out, x_tiles = outs
    for i in range(2):
        out[i * 128 : (i + 1) * 128, :] = up1[i]
        out[256 + i * 128 : 256 + (i + 1) * 128, :] = ds[i]
        out[512 + i * 512 : 512 + (i + 1) * 512, :] = d1[i]
        for cq in range(4):
            row = 1536 + (i * 4 + cq) * 128
            out[row : row + 128, :] = up2[i, :, cq * 128 : (cq + 1) * 128]
    for a in range(4):
        x_out[a] = x_ref[a]
        pack_quarter(x_ref[a].astype(F32), a, packed, temp)
    x_tiles[...] = narrow(packed)


def first_rows_body(ins, outs, packed, temp):
    x_ref, x_tiles, key_mine, key_got, mine_ref, got_ref = ins
    g = core()
    key = jnp.where(g == 0, key_mine[...], key_got[...])
    for a in range(4):
        factor = jnp.where(g == 0, mine_ref[a], got_ref[4 * g + a])
        scaled = (x_ref[a].astype(F32) * key).astype(BF)
        pack_quarter(dot(factor, scaled), a, packed, temp)
    outs[0][...] = joined(packed, x_tiles)


def weights_body(layer, ins, outs):
    g, m = core(), side()
    own_ref, peer_ref, other_ref, both_ref = ins[:4]
    u_ref, v_ref, up2_ref, d1_ref = (o.ref for o in outs[:4])

    def block(start, rows, mine):
        part = slice(start, start + rows)
        here = jnp.where(mine, own_ref[part, :], peer_ref[part, :])
        there = jnp.where(mine, other_ref[part, :], both_ref[part, :])
        return jnp.where(g == layer, here, there)

    rho = lax.broadcasted_iota(jnp.int32, (128, 512), 0)
    gam = lax.broadcasted_iota(jnp.int32, (128, 512), 1)
    same = (gam // 128) * 32 + gam % 32 == rho
    for k in range(4):
        i, mine = k % 2, m == k // 2
        spot = jnp.where(same & ((gam // 32) % 4 == k), 1.0, 0.0).astype(BF)
        u_ref[k * 128 : (k + 1) * 128, :] = dot(block(i * 128, 128, mine), spot).astype(BF)
        spread = lax.dot_general(
            spot, block(256 + i * 128, 128, mine), (((0,), (0,)), ((), ())),
            preferred_element_type=F32,
        )
        v_ref[:, k * 128 : (k + 1) * 128] = spread.astype(BF)
        d1_ref[k] = block(512 + i * 512, 512, mine)
        for cq in range(4):
            up2_ref[k, :, cq * 128 : (cq + 1) * 128] = block(1536 + (i * 4 + cq) * 128, 128, mine)
        for out in outs[2:4]:
            out.send(k)
    if layer == 1:
        return
    own, peer, other, both = (n[...] for n in ins[6:10])
    for half in range(2):
        lanes = slice(half * 256, (half + 1) * 256)
        mine = jnp.where(m == half, own, peer)
        got = jnp.where(m == half, other, both)
        outs[4].ref[:, lanes] = jnp.where(g == 0, mine, got)
        outs[5].ref[:, lanes] = jnp.where(g == 0, got, mine)
    for oo in range(2):
        outs[6].ref[oo] = jnp.where(g == 0, ins[4][oo], ins[5][oo])


def factors_body(ins, outs):
    g = core()
    first_mine, first_got, second_mine, second_got = ins
    first1, first1_t, second1, second1_t, second0_t = (o.ref for o in outs)
    for i in range(2):
        first = jnp.where(g == 1, first_mine[i], first_got[i])
        first1[i] = first
        first1_t[i] = first.astype(F32).T.astype(BF)
        second = jnp.where(g == 1, second_mine[i], second_got[i])
        second1[i] = second
        second1_t[i] = second.astype(F32).T.astype(BF)
        second = jnp.where(g == 0, second_mine[i], second_got[i])
        second0_t[i] = second.astype(F32).T.astype(BF)


def forward_cols_body(ins, outs, wide, wide_x, packed):
    msg, factor, gains0, gains1, u, up2, down1, v = ins
    out_msg, mixed_out, x_out, hidden_out, middle_out = outs
    parted(msg, wide, wide_x)
    for oo in range(2):
        mixed = unpack_quarter(wide, oo).astype(BF)
        x = unpack_quarter(wide_x, oo)
        turned = dot(factor[oo], mixed).astype(BF)
        pre = x * gains0[0:1, :]
        hidden = (x + pre * sigmoid(pre) * turned.astype(F32)).astype(BF)
        for out, value in ((mixed_out, mixed), (x_out, x.astype(BF)), (hidden_out, hidden)):
            out.ref[oo] = value
            out.send(oo)
        permuted = dot(hidden, u[...]).astype(BF)
        folds = []
        for j in range(4):
            preact = dot(permuted[:, j * 128 : (j + 1) * 128], up2[j])
            active = (preact * sigmoid(preact)).astype(BF)
            folds.append(dot(active, down1[j]).astype(BF))
        out = dot(jnp.concatenate(folds, axis=1), v[...])
        middle = (hidden.astype(F32) + out).astype(BF)
        middle_out.ref[oo] = middle
        middle_out.send(oo)
        pack_cols(middle.astype(F32) * gains1[1:2, :], oo, packed)
    out_msg[...] = narrow(packed)


def rows_body(ins, outs, wide, packed, temp, temp4):
    msg, factor, more = ins
    widen(msg, wide)
    for a2 in range(2):
        values = unpack_rows(wide, a2, temp4).astype(BF)
        outs[1].ref[a2] = values
        outs[1].send(a2)
        result = dot(factor[a2], values)
        if outs[0].shape == MSG:
            result = result * more[1:2, :]
        pack_rows(result, a2, packed, temp)
    if outs[0].shape == MSG:
        outs[0][...] = narrow(packed)
    else:
        outs[0][...] = joined(packed, more)


def grad_body(ins, outs):
    outer, inner = ins
    for i in range(2):
        grad = dot_nt(outer[i], inner[i]).astype(BF)
        outs[0].ref[0, i] = grad[:128]
        outs[0].ref[1, i] = grad[128:]


def second_grads_body(ins, outs, own, other):
    g, m = core(), side()
    outer, inner, upper = ins
    for i in range(2):
        grad = dot_nt(outer[i], inner[i]).astype(BF)
        for half in range(2):
            lower = grad[half * 128 : (half + 1) * 128]
            own[half, i] = jnp.where(g == 0, lower, upper[half, i])
            other[half, i] = jnp.where(g == 0, upper[half, i], lower)
    for out, (source, half) in zip(outs, ((own, m), (own, 1 - m), (other, m), (other, 1 - m))):
        out[...] = source[half]


def last_rows_body(ins, outs, wide, temp4):
    msg, x_own, x_peer, gains, upper = ins
    m = side()
    widen(msg, wide)
    for a2 in range(2):
        values = unpack_rows(wide, a2, temp4).astype(BF)
        own, peer = x_own[a2].astype(F32), x_peer[a2].astype(F32)
        low = (jnp.where(m == 0, own, peer) * gains[1:2, :256]).astype(BF)
        high = (jnp.where(m == 0, peer, own) * gains[1:2, 256:]).astype(BF)
        grad = dot_nt(values[:, :256], low) + dot_nt(values[:, 256:], high)
        outs[0][0, a2] = grad[:128].astype(BF)
        outs[0][1, a2] = grad[128:].astype(BF)
    for half in range(2):
        outs[0][2 + half] = upper[half]


def collect_body(ins, outs):
    g, m = core(), side()
    owners = 2 * g + m, 2 * (1 - g) + m, 2 * g + 1 - m, 2 * (1 - g) + 1 - m
    for n, owner in enumerate(owners):
        part = pl.ds(2 * owner, 2)
        outs[0].ref[part] = ins[n][...].astype(F32)
        outs[0].send(part)


def ffn_back(cot, hidden, u, v, up2, down1):
    permuted = dot(hidden, u[...]).astype(BF)
    fold = dot_nt(cot, v[...]).astype(BF)
    perms = []
    for j in range(4):
        block = slice(j * 128, (j + 1) * 128)
        preact = dot(permuted[:, block], up2[j])
        back_active = dot_nt(fold[:, block], down1[j])
        back_preact = (back_active * slope(preact)).astype(BF)
        perms.append(dot_nt(back_preact, up2[j]).astype(BF))
    return cot.astype(F32) + dot_nt(jnp.concatenate(perms, axis=1), u[...])


def upper_cols_body(ins, outs, wide, wide_c, packed, temp4):
    msg, factor, x_ref, gains, v, u, up2, down1, factor_t = ins
    out_msg, mixed_out, back_turned_out, direct_out = outs
    parted(msg, wide, wide_c)
    for oo in range(2):
        mixed = unpack_cols(wide, oo).astype(BF)
        cot = unpack_quarter_rows(wide_c, oo, temp4).astype(BF)
        mixed_out.ref[oo] = mixed
        mixed_out.send(oo)
        gate = gains[0:1, :]
        x = x_ref[oo].astype(F32)
        turned = dot(factor[oo], mixed).astype(BF).astype(F32)
        pre = x * gate
        logistic = sigmoid(pre)
        gated = pre * logistic
        hidden = (x + gated * turned).astype(BF)
        back_hidden = ffn_back(cot, hidden, u, v, up2, down1)
        back_turned = (back_hidden * gated).astype(BF)
        back_turned_out.ref[oo] = back_turned
        back_turned_out.send(oo)
        gate_slope = logistic * (1.0 + pre * (1.0 - logistic))
        direct_out.ref[oo] = back_hidden + back_hidden * turned * gate_slope * gate
        direct_out.send(oo)
        pack_cols(dot(factor_t[oo], back_turned), oo, packed)
    out_msg[...] = narrow(packed)


def lower_cols_body(ins, outs, wide, packed):
    msg, direct0, hidden_ref, v, u, up2, down1, direct1, x_ref, gains, factor_t = ins
    direct = direct0, direct1
    out_msg, back_turned_out = outs
    widen(msg, wide)
    for oo in range(2):
        passed = (direct[oo][...] + unpack_cols(wide, oo)).astype(BF)
        back_hidden = ffn_back(passed, hidden_ref[oo], u, v, up2, down1)
        pre = x_ref[oo].astype(F32) * gains[0:1, :]
        back_turned = (back_hidden * (pre * sigmoid(pre))).astype(BF)
        back_turned_out.ref[oo] = back_turned
        back_turned_out.send(oo)
        pack_cols(dot(factor_t[oo], back_turned), oo, packed)
    out_msg[...] = narrow(packed)


def layer_pair(
    inputs,
    cotangent,
    gate_gain,
    key_gain,
    first_factor,
    second_factor,
    up_first,
    up_second,
    down_first,
    down_second_weight,
):
    g, m = core(), side()
    rows = inputs.reshape(8, 256, 256)
    cot_rows = cotangent.reshape(8, 256, 256)
    first_mine, second_mine = first_factor[0], second_factor[0]
    seq_count = lax.axis_size("seq")

    def swap_z(value, layers):
        pairs = [
            ((layer * seq_count + q) * 2 + end, (layer * seq_count + (q ^ (seq_count // 2))) * 2 + 1 - end)
            for layer in layers
            for q in range(seq_count)
            for end in range(2)
        ]
        return lax.ppermute(value, ("segment", "seq", "mp"), pairs)

    def give(value, layer):
        return lax.ppermute(value, "segment", [(layer, 1 - layer)])

    def two(array):
        def view(ref):
            return ref.at[pl.ds(2 * (2 * core() + side()), 2)]

        return array, view, (2,) + array.shape[1:]

    def four(array):
        def view(ref):
            return ref.at[pl.ds(4 * core(), 4)]

        return array, view, (4,) + array.shape[1:]

    def part(array, n):
        return array, lambda ref: ref.at[n], array.shape[1:]

    tiles = Near((MSG, BF))
    scratch_pack = [(MSG, F32), ((256, 128), F32)]

    key_got = swap(key_gain, "segment")
    own, x_rows, x_tiles = call(
        pack_body,
        [Near(((WEIGHT_ROWS, 128), BF)), Near(((4, 256, 256), BF)), tiles],
        scratch_pack,
        (four(rows), up_first[0], down_second_weight[0], down_first[0], up_second[0]),
    )
    first_got = swap(first_mine, "segment")
    peer0 = swap_z(own, (0,))
    (rows_msg,) = call(
        first_rows_body,
        [Near((PAIR, BF))],
        scratch_pack,
        (Near(x_rows), Near(x_tiles), key_gain, key_got, Near(first_mine), Near(first_got)),
    )

    def send(message, order=ROWS_ORDER):
        return exchange(message, order)

    msg = send(rows_msg, QUARTER_ORDER)

    second_got = swap(second_mine, "segment")
    gains = jnp.concatenate([gate_gain, key_gain])
    gains_peer = swap_z(gains, (0, 1))
    gains_got = swap(gains, "segment")
    gains_both = swap(gains_peer, "segment")
    other0 = give(own, 0)
    both0 = give(peer0, 0)
    square = ((512, 512), BF)
    layer_outs = [square, square, ((4, 128, 512), BF), ((4, 512, 128), BF)]
    gain = ((2, 512), F32)
    pair = ((2, 256, 256), BF)
    u0, v0, up0, down0, gains0, gains1, second0 = call(
        lambda ins, outs: weights_body(0, ins, outs),
        layer_outs + [gain, gain, pair],
        [],
        (
            own, peer0, other0, both0, two(second_mine), two(second_got),
            gains, gains_peer, gains_got, gains_both,
        ),
    )

    block = ((2, 256, 512), BF)
    next_msg, mixed0, x0, hidden0, middle = call(
        forward_cols_body,
        [tiles] + [block] * 4,
        [(MSG, F32)] * 3,
        (Near(msg), second0, gains0, gains1, u0, up0, down0, v0),
    )
    msg = send(next_msg)
    peer1 = swap_z(own, (1,))
    other1 = give(own, 1)
    first1, first1_t, second1, second1_t, second0_t = call(
        factors_body,
        [pair] * 5,
        [],
        (two(first_mine), two(first_got), two(second_mine), two(second_got)),
        after=(next_msg,),
    )
    (cot_tiles,) = call(pack_cot_body, [tiles], scratch_pack, (four(cot_rows),), after=(first1,))

    scratch_rows = [(MSG, F32), (MSG, F32), ((256, 128), F32), ((4, 256, 128), F32)]
    next_msg, scaled1 = call(
        rows_body, [Near((PAIR, BF)), block], scratch_rows, (Near(msg), first1, Near(cot_tiles))
    )
    msg = send(next_msg)
    both1 = give(peer1, 1)
    u1, v1, up1, down1 = call(
        lambda ins, outs: weights_body(1, ins, outs), layer_outs, [], (own, peer1, other1, both1)
    )
    next_msg, mixed1, back_turned1, direct = call(
        upper_cols_body,
        [tiles, block, block, ((2, 256, 512), F32)],
        [(MSG, F32)] * 3 + [((4, 256, 128), F32)],
        (Near(msg), second1, middle, gains1, v1, u1, up1, down1, second1_t),
    )
    msg = send(next_msg)

    halves = ((2, 2, 128, 256), BF)

    def channel_grad(outer, inner, after):
        (grad,) = call(grad_body, [halves], [], (outer, inner), after=(after,))
        return grad

    second_grad1 = channel_grad(back_turned1, mixed1, next_msg)

    next_msg, back_rows1 = call(
        rows_body, [tiles, block], scratch_rows, (Near(msg), first1_t, gains1)
    )
    msg = send(next_msg)
    first_grad1 = channel_grad(back_rows1, scaled1, next_msg)

    (x_sent,) = call(
        slice_body,
        [((2, 256, 256), BF)],
        [],
        ((rows, lambda ref: ref.at[pl.ds(2 * (2 * core() + 1 - side()), 2)], (2, 256, 256)),),
        after=(first_grad1,),
    )
    x_peer = swap(x_sent, "mp")

    next_msg, back_turned0 = call(
        lower_cols_body,
        [tiles, block],
        [(MSG, F32)] * 2,
        (Near(msg), part(direct, 0), hidden0, v0, u0, up0, down0, part(direct, 1), x0, gains0, second0_t),
    )
    msg = send(next_msg)
    half = Near(((2, 128, 256), BF))
    mine, own_theirs, other_mine, other_theirs = call(
        second_grads_body,
        [half] * 4,
        [halves] * 2,
        (back_turned0, mixed0, second_grad1),
        after=(next_msg,),
    )
    from_side = swap(own_theirs, "mp")
    from_both = lax.ppermute(other_theirs, ("segment", "mp"), [(0, 3), (1, 2), (2, 1), (3, 0)])
    from_core = swap(other_mine, "segment")

    (message,) = call(
        last_rows_body,
        [Near(((4, 2, 128, 256), BF))],
        [(MSG, F32), ((4, 256, 128), F32)],
        (Near(msg), two(rows), x_peer, gains0, first_grad1),
    )
    grad_first = lax.all_to_all(message, ("segment", "mp"), split_axis=0, concat_axis=0, tiled=True)
    (grad_second,) = call(
        collect_body,
        [((8, 128, 256), F32)],
        [],
        (mine, from_core, from_side, from_both),
        after=(message,),
    )
    return grad_first.reshape(1, 8, 128, 256).astype(F32), grad_second[None]


def solution(mesh):
    placed = (
        P("seq", "mp"),
        P("seq", "mp"),
        P("segment", "mp"),
        P("segment", "mp"),
        P("segment", "seq", None, None),
        P("segment", "seq", None, None),
        P("segment", "mp", None, None),
        P("segment", "mp", None, None),
        P("segment", "mp", None, None),
        P("segment", "mp", None, None),
    )
    return jax.shard_map(
        layer_pair,
        mesh=mesh,
        in_specs=placed,
        out_specs=(P("segment", "seq", "mp", None), P("segment", "seq", "mp", None)),
        check_vma=False,
    )
```

```python
import math

import jax
import jax.numpy as jnp
from jax import lax
from jax.experimental import pallas as pl
from jax.experimental.pallas import tpu as pltpu
from jax.sharding import PartitionSpec as P


ROWS_ORDER = ("seq", "segment", "mp")
QUARTER_ORDER = ("mp", "seq", "segment")
BF = jnp.bfloat16
F32 = jnp.float32
MSG = (2048, 128)
OWNERS = 128
PAIR = (4096, 128)
VMEM_BYTES = 67043328
SPARE = 16 * 2**20
WEIGHT_ROWS = 2560


def exchange(message, order):
    return lax.all_to_all(message, order, split_axis=0, concat_axis=0, tiled=True)


def swap(value, axis):
    return lax.ppermute(value, axis, [(0, 1), (1, 0)])


def dot(a, b):
    return jnp.dot(a, b, preferred_element_type=F32)


def dot_nt(a, b):
    return lax.dot_general(a, b, (((1,), (1,)), ((), ())), preferred_element_type=F32)


def sigmoid(v):
    return 0.5 * jnp.tanh(0.5 * v) + 0.5


def slope(v):
    s = sigmoid(v)
    return s * (1.0 + v * (1.0 - s))


class Loaded:
    def __init__(self, source, buffer, sem):
        self.copy, self.buffer, self.ready = pltpu.make_async_copy(source, buffer, sem), buffer, False
        self.copy.start()

    def get(self):
        if not self.ready:
            self.copy.wait()
            self.ready = True
        return self.buffer

    def __getitem__(self, index):
        return self.get()[index]


class Result:
    def __init__(self, target, buffer, sems):
        self.target, self.ref, self.sems, self.copies = target, buffer, sems, []

    def send(self, *index):
        source, target = (self.ref.at[index], self.target.at[index]) if index else (self.ref, self.target)
        copy = pltpu.make_async_copy(source, target, self.sems.at[len(self.copies)])
        copy.start()
        self.copies.append(copy)


class Near:
    def __init__(self, value):
        self.value = value


def call(body, outs, scratch, args, after=()):
    near_in = [isinstance(a, Near) for a in args]
    near_out = [isinstance(o, Near) for o in outs]
    args = [a.value if isinstance(a, Near) else a for a in args]
    args = [a if isinstance(a, tuple) else (a, None, a.shape) for a in args]
    outs = [o.value if isinstance(o, Near) else o for o in outs]
    far_in = [n for n, near in enumerate(near_in) if not near]
    far_out = [n for n, near in enumerate(near_out) if not near]
    total = len(args) + len(after)

    def kernel(*refs):
        sources, targets = refs[: len(args)], refs[total : total + len(outs)]
        rest = refs[total + len(outs) :]
        buffers, rest = rest[: len(far_in)], rest[len(far_in) :]
        results, rest = rest[: len(far_out)], rest[len(far_out) :]
        sems, out_sems, *extra = rest
        loads, stores = list(sources), list(targets)
        for k, n in enumerate(far_in):
            view = args[n][1]
            loads[n] = Loaded(view(sources[n]) if view else sources[n], buffers[k], sems.at[k])
        for k, n in enumerate(far_out):
            stores[n] = Result(targets[n], results[k], out_sems.at[k])
        body(loads, stores, *extra)
        for n in far_in:
            loads[n].get()
        for n in far_out:
            if not stores[n].copies:
                stores[n].send()
        for n in far_out:
            for copy in stores[n].copies:
                copy.wait()

    moved = sum(math.prod(shape) * a.dtype.itemsize for a, view, shape in args)
    moved += sum(math.prod(shape) * jnp.dtype(dtype).itemsize for shape, dtype in outs)
    held = sum(math.prod(args[n][0].shape) * args[n][0].dtype.itemsize for n in range(len(args)) if near_in[n])
    held += sum(math.prod(outs[n][0]) * jnp.dtype(outs[n][1]).itemsize for n in range(len(outs)) if near_out[n])
    near, far = pl.BlockSpec(memory_space=pltpu.VMEM), pl.BlockSpec(memory_space=pltpu.HBM)
    return pl.pallas_call(
        kernel,
        out_shape=tuple(
            jax.ShapeDtypeStruct(*o) if n else pltpu.HBM(*o) for n, o in zip(near_out, outs)
        ),
        in_specs=[near if n else far for n in near_in]
        + [pl.BlockSpec(memory_space=pl.ANY)] * len(after),
        out_specs=tuple(near if n else far for n in near_out),
        scratch_shapes=[pltpu.VMEM(args[n][2], args[n][0].dtype) for n in far_in]
        + [pltpu.VMEM(*outs[n]) for n in far_out]
        + [pltpu.SemaphoreType.DMA((max(1, len(far_in)),)), pltpu.SemaphoreType.DMA((max(1, len(far_out)), 8))]
        + [pltpu.VMEM(s, d) for s, d in scratch],
        compiler_params=pltpu.CompilerParams(vmem_limit_bytes=VMEM_BYTES - held - SPARE),
        cost_estimate=pl.CostEstimate(flops=10**8, bytes_accessed=moved, transcendentals=0),
    )(
        *[a[0] if n else pltpu.with_memory_space_constraint(a[0], pltpu.HBM) for n, a in zip(near_in, args)],
        *after,
    )


def core():
    return lax.axis_index("segment")


def side():
    return lax.axis_index("mp")


def widen(msg, wide):
    wide[...] = msg[...].astype(F32)


def narrow(packed):
    return packed[...].astype(BF)


def joined(packed, tiles):
    parts = [values.reshape(OWNERS, 16, 128) for values in (packed[...], tiles[...].astype(F32))]
    return jnp.concatenate(parts, axis=1).reshape(PAIR).astype(BF)


def parted(msg, wide, wide_more):
    both = msg[...].astype(F32).reshape(OWNERS, 32, 128)
    wide[...] = both[:, :16].reshape(MSG)
    wide_more[...] = both[:, 16:].reshape(MSG)


def pack_quarter(values, a, out, temp):
    for h in range(2):
        temp[...] = values[:, h * 128 : (h + 1) * 128]
        for mm in range(2):
            for oo in range(2):
                row = mm * 1024 + a * 4 + oo * 2 + h
                out[pl.ds(row, 64, stride=16), :] = temp[pl.ds(mm * 2 + oo, 64, stride=4), :]


def unpack_quarter(source, oo):
    parts = [
        source[pl.ds(mm * 1024 + oo * 2 + h, 256, stride=4), :] for mm in range(2) for h in range(2)
    ]
    return jnp.concatenate(parts, axis=1)


def pack_quarter_rows(values, a, out, temp):
    for h in range(2):
        temp[...] = values[:, h * 128 : (h + 1) * 128]
        for oo in range(2):
            out[pl.ds(a * 4 + oo * 2 + h, 128, stride=16), :] = temp[pl.ds(oo, 128, stride=2), :]


def unpack_quarter_rows(source, oo, temp):
    for mm in range(2):
        for h in range(2):
            for a in range(4):
                temp[mm * 2 + h, pl.ds(a, 64, stride=4), :] = source[
                    pl.ds(mm * 16 + a * 4 + oo * 2 + h, 64, stride=32), :
                ]
    return jnp.concatenate([temp[n] for n in range(4)], axis=1)


def pack_cols(values, oo, out):
    for cq in range(4):
        out[pl.ds(oo * 4 + cq, 256, stride=8), :] = values[:, cq * 128 : (cq + 1) * 128]


def unpack_cols(source, oo):
    return jnp.concatenate(
        [source[pl.ds(oo * 4 + cq, 256, stride=8), :] for cq in range(4)], axis=1
    )


def pack_rows(values, a2, out, temp):
    for cq in range(4):
        temp[...] = values[:, cq * 128 : (cq + 1) * 128]
        for oo in range(2):
            out[pl.ds(a2 * 8 + oo * 4 + cq, 128, stride=16), :] = temp[pl.ds(oo, 128, stride=2), :]


def unpack_rows(source, a2, temp):
    for cq in range(4):
        for oo in range(2):
            temp[cq, pl.ds(oo, 128, stride=2), :] = source[
                pl.ds(a2 * 8 + oo * 4 + cq, 128, stride=16), :
            ]
    return jnp.concatenate([temp[cq] for cq in range(4)], axis=1)


def slice_body(ins, outs):
    outs[0].ref[...] = ins[0][...]


def pack_cot_body(ins, outs, packed, temp):
    (x_ref,) = ins
    for a in range(4):
        pack_quarter_rows(x_ref[a].astype(F32), a, packed, temp)
    outs[0][...] = narrow(packed)


def pack_body(ins, outs, packed, temp):
    x_ref, up1, ds, d1, up2, gate, key = ins
    out, x_out, x_tiles, gains = outs
    gains[0:1, :] = gate[...]
    gains[1:2, :] = key[...]
    for i in range(2):
        out[i * 128 : (i + 1) * 128, :] = up1[i]
        out[256 + i * 128 : 256 + (i + 1) * 128, :] = ds[i]
        out[512 + i * 512 : 512 + (i + 1) * 512, :] = d1[i]
        for cq in range(4):
            row = 1536 + (i * 4 + cq) * 128
            out[row : row + 128, :] = up2[i, :, cq * 128 : (cq + 1) * 128]
    for a in range(4):
        x_out[a] = x_ref[a]
        pack_quarter(x_ref[a].astype(F32), a, packed, temp)
    x_tiles[...] = narrow(packed)


def first_rows_body(ins, outs, packed, temp):
    x_ref, x_tiles, gains, key_got, mine_ref, got_ref = ins
    g = core()
    key = jnp.where(g == 0, gains[1:2, :], key_got[...])
    for a in range(4):
        factor = jnp.where(g == 0, mine_ref[a], got_ref[4 * g + a])
        scaled = (x_ref[a].astype(F32) * key).astype(BF)
        pack_quarter(dot(factor, scaled), a, packed, temp)
    outs[0][...] = joined(packed, x_tiles)


def weights_body(layer, ins, outs):
    g, m = core(), side()
    own_ref, peer_ref, other_ref, both_ref = ins[:4]
    u_ref, v_ref, up2_ref, d1_ref = (o.ref for o in outs[:4])

    def block(start, rows, mine):
        part = slice(start, start + rows)
        here = jnp.where(mine, own_ref[part, :], peer_ref[part, :])
        there = jnp.where(mine, other_ref[part, :], both_ref[part, :])
        return jnp.where(g == layer, here, there)

    rho = lax.broadcasted_iota(jnp.int32, (128, 512), 0)
    gam = lax.broadcasted_iota(jnp.int32, (128, 512), 1)
    same = (gam // 128) * 32 + gam % 32 == rho
    for k in range(4):
        i, mine = k % 2, m == k // 2
        spot = jnp.where(same & ((gam // 32) % 4 == k), 1.0, 0.0).astype(BF)
        u_ref[k * 128 : (k + 1) * 128, :] = dot(block(i * 128, 128, mine), spot).astype(BF)
        spread = lax.dot_general(
            spot, block(256 + i * 128, 128, mine), (((0,), (0,)), ((), ())),
            preferred_element_type=F32,
        )
        v_ref[:, k * 128 : (k + 1) * 128] = spread.astype(BF)
        d1_ref[k] = block(512 + i * 512, 512, mine)
        for cq in range(4):
            up2_ref[k, :, cq * 128 : (cq + 1) * 128] = block(1536 + (i * 4 + cq) * 128, 128, mine)
        for out in outs[2:4]:
            out.send(k)
    if layer == 1:
        return
    own, peer, other, both = (n[...] for n in ins[6:10])
    for half in range(2):
        lanes = slice(half * 256, (half + 1) * 256)
        mine = jnp.where(m == half, own, peer)
        got = jnp.where(m == half, other, both)
        outs[4].ref[:, lanes] = jnp.where(g == 0, mine, got)
        outs[5].ref[:, lanes] = jnp.where(g == 0, got, mine)
    for oo in range(2):
        outs[6].ref[oo] = jnp.where(g == 0, ins[4][oo], ins[5][oo])


def factors_body(ins, outs):
    g = core()
    first_mine, first_got, second_mine, second_got = ins
    first1, first1_t, second1, second1_t, second0_t = (o.ref for o in outs)
    for i in range(2):
        first = jnp.where(g == 1, first_mine[i], first_got[i])
        first1[i] = first
        first1_t[i] = first.astype(F32).T.astype(BF)
        second = jnp.where(g == 1, second_mine[i], second_got[i])
        second1[i] = second
        second1_t[i] = second.astype(F32).T.astype(BF)
        second = jnp.where(g == 0, second_mine[i], second_got[i])
        second0_t[i] = second.astype(F32).T.astype(BF)


def forward_cols_body(ins, outs, wide, wide_x, packed):
    msg, factor, gains0, gains1, u, up2, down1, v = ins
    out_msg, mixed_out, x_out, hidden_out, middle_out = outs
    parted(msg, wide, wide_x)
    for oo in range(2):
        mixed = unpack_quarter(wide, oo).astype(BF)
        x = unpack_quarter(wide_x, oo)
        turned = dot(factor[oo], mixed).astype(BF)
        pre = x * gains0[0:1, :]
        hidden = (x + pre * sigmoid(pre) * turned.astype(F32)).astype(BF)
        for out, value in ((mixed_out, mixed), (x_out, x.astype(BF)), (hidden_out, hidden)):
            out.ref[oo] = value
            out.send(oo)
        permuted = dot(hidden, u[...]).astype(BF)
        folds = []
        for j in range(4):
            preact = dot(permuted[:, j * 128 : (j + 1) * 128], up2[j])
            active = (preact * sigmoid(preact)).astype(BF)
            folds.append(dot(active, down1[j]).astype(BF))
        out = dot(jnp.concatenate(folds, axis=1), v[...])
        middle = (hidden.astype(F32) + out).astype(BF)
        middle_out.ref[oo] = middle
        middle_out.send(oo)
        pack_cols(middle.astype(F32) * gains1[1:2, :], oo, packed)
    out_msg[...] = narrow(packed)


def rows_body(ins, outs, wide, packed, temp, temp4):
    msg, factor, more = ins
    widen(msg, wide)
    for a2 in range(2):
        values = unpack_rows(wide, a2, temp4).astype(BF)
        outs[1].ref[a2] = values
        outs[1].send(a2)
        result = dot(factor[a2], values)
        if outs[0].shape == MSG:
            result = result * more[1:2, :]
        pack_rows(result, a2, packed, temp)
    if outs[0].shape == MSG:
        outs[0][...] = narrow(packed)
    else:
        outs[0][...] = joined(packed, more)


def grad_body(ins, outs):
    outer, inner = ins
    for i in range(2):
        grad = dot_nt(outer[i], inner[i]).astype(BF)
        outs[0].ref[0, i] = grad[:128]
        outs[0].ref[1, i] = grad[128:]


def second_grads_body(ins, outs, own, other):
    g, m = core(), side()
    outer, inner, upper = ins
    for i in range(2):
        grad = dot_nt(outer[i], inner[i]).astype(BF)
        for half in range(2):
            lower = grad[half * 128 : (half + 1) * 128]
            own[half, i] = jnp.where(g == 0, lower, upper[half, i])
            other[half, i] = jnp.where(g == 0, upper[half, i], lower)
    for out, (source, half) in zip(outs, ((own, m), (own, 1 - m), (other, m), (other, 1 - m))):
        out[...] = source[half]


def last_rows_body(ins, outs, wide, temp4):
    msg, x_own, x_peer, gains, upper = ins
    m = side()
    widen(msg, wide)
    for a2 in range(2):
        values = unpack_rows(wide, a2, temp4).astype(BF)
        own, peer = x_own[a2].astype(F32), x_peer[a2].astype(F32)
        low = (jnp.where(m == 0, own, peer) * gains[1:2, :256]).astype(BF)
        high = (jnp.where(m == 0, peer, own) * gains[1:2, 256:]).astype(BF)
        grad = dot_nt(values[:, :256], low) + dot_nt(values[:, 256:], high)
        outs[0][0, a2] = grad[:128].astype(BF)
        outs[0][1, a2] = grad[128:].astype(BF)
    for half in range(2):
        outs[0][2 + half] = upper[half]


def collect_body(ins, outs):
    g, m = core(), side()
    owners = 2 * g + m, 2 * (1 - g) + m, 2 * g + 1 - m, 2 * (1 - g) + 1 - m
    for n, owner in enumerate(owners):
        part = pl.ds(2 * owner, 2)
        outs[0].ref[part] = ins[n][...].astype(F32)
        outs[0].send(part)


def slope_body(ins, outs):
    hidden, u, up2 = ins
    for oo in range(2):
        permuted = dot(hidden[oo], u[...]).astype(BF)
        for j in range(4):
            block = slice(j * 128, (j + 1) * 128)
            outs[0].ref[oo, j] = slope(dot(permuted[:, block], up2[j])).astype(BF)
        outs[0].send(oo)


def ffn_back(cot, slope_of, u, v, up2, down1):
    fold = dot_nt(cot, v[...]).astype(BF)
    perms = []
    for j in range(4):
        block = slice(j * 128, (j + 1) * 128)
        back_active = dot_nt(fold[:, block], down1[j])
        back_preact = (back_active * slope_of(j)).astype(BF)
        perms.append(dot_nt(back_preact, up2[j]).astype(BF))
    return cot.astype(F32) + dot_nt(jnp.concatenate(perms, axis=1), u[...])


def upper_cols_body(ins, outs, wide, wide_c, packed, temp4):
    msg, factor, x_ref, gains, v, u, up2, down1, factor_t = ins
    out_msg, mixed_out, back_turned_out, direct_out = outs
    parted(msg, wide, wide_c)
    for oo in range(2):
        mixed = unpack_cols(wide, oo).astype(BF)
        cot = unpack_quarter_rows(wide_c, oo, temp4).astype(BF)
        mixed_out.ref[oo] = mixed
        mixed_out.send(oo)
        gate = gains[0:1, :]
        x = x_ref[oo].astype(F32)
        turned = dot(factor[oo], mixed).astype(BF).astype(F32)
        pre = x * gate
        logistic = sigmoid(pre)
        gated = pre * logistic
        hidden = (x + gated * turned).astype(BF)
        permuted = dot(hidden, u[...]).astype(BF)

        def slope_of(j):
            return slope(dot(permuted[:, j * 128 : (j + 1) * 128], up2[j]))

        back_hidden = ffn_back(cot, slope_of, u, v, up2, down1)
        back_turned = (back_hidden * gated).astype(BF)
        back_turned_out.ref[oo] = back_turned
        back_turned_out.send(oo)
        gate_slope = logistic * (1.0 + pre * (1.0 - logistic))
        direct_out.ref[oo] = back_hidden + back_hidden * turned * gate_slope * gate
        direct_out.send(oo)
        pack_cols(dot(factor_t[oo], back_turned), oo, packed)
    out_msg[...] = narrow(packed)


def lower_cols_body(ins, outs, wide, packed):
    msg, direct0, v, down1, slopes0, up2, u, x_ref, gains, direct1, slopes1, factor_t = ins
    direct, slopes = (direct0, direct1), (slopes0, slopes1)
    out_msg, back_turned_out = outs
    widen(msg, wide)
    for oo in range(2):
        passed = (direct[oo][...] + unpack_cols(wide, oo)).astype(BF)
        back_hidden = ffn_back(passed, lambda j: slopes[oo][j].astype(F32), u, v, up2, down1)
        pre = x_ref[oo].astype(F32) * gains[0:1, :]
        back_turned = (back_hidden * (pre * sigmoid(pre))).astype(BF)
        back_turned_out.ref[oo] = back_turned
        back_turned_out.send(oo)
        pack_cols(dot(factor_t[oo], back_turned), oo, packed)
    out_msg[...] = narrow(packed)


def layer_pair(
    inputs,
    cotangent,
    gate_gain,
    key_gain,
    first_factor,
    second_factor,
    up_first,
    up_second,
    down_first,
    down_second_weight,
):
    g, m = core(), side()
    rows = inputs.reshape(8, 256, 256)
    cot_rows = cotangent.reshape(8, 256, 256)
    first_mine, second_mine = first_factor[0], second_factor[0]
    seq_count = lax.axis_size("seq")

    def swap_z(value, layers):
        pairs = [
            ((layer * seq_count + q) * 2 + end, (layer * seq_count + (q ^ (seq_count // 2))) * 2 + 1 - end)
            for layer in layers
            for q in range(seq_count)
            for end in range(2)
        ]
        return lax.ppermute(value, ("segment", "seq", "mp"), pairs)

    def give(value, layer):
        return lax.ppermute(value, "segment", [(layer, 1 - layer)])

    def two(array):
        def view(ref):
            return ref.at[pl.ds(2 * (2 * core() + side()), 2)]

        return array, view, (2,) + array.shape[1:]

    def four(array):
        def view(ref):
            return ref.at[pl.ds(4 * core(), 4)]

        return array, view, (4,) + array.shape[1:]

    def part(array, n):
        return array, lambda ref: ref.at[n], array.shape[1:]

    tiles = Near((MSG, BF))
    scratch_pack = [(MSG, F32), ((256, 128), F32)]

    key_got = swap(key_gain, "segment")
    own, x_rows, x_tiles, gains = call(
        pack_body,
        [Near(((WEIGHT_ROWS, 128), BF)), Near(((4, 256, 256), BF)), tiles, Near(((2, 256), F32))],
        scratch_pack,
        (four(rows), up_first[0], down_second_weight[0], down_first[0], up_second[0], gate_gain, key_gain),
    )
    first_got = swap(first_mine, "segment")
    peer0 = swap_z(own, (0,))
    (rows_msg,) = call(
        first_rows_body,
        [Near((PAIR, BF))],
        scratch_pack,
        (Near(x_rows), Near(x_tiles), Near(gains), Near(key_got), Near(first_mine), Near(first_got)),
    )

    def send(message, order=ROWS_ORDER):
        return exchange(message, order)

    msg = send(rows_msg, QUARTER_ORDER)

    second_got = swap(second_mine, "segment")
    gains_peer = swap_z(gains, (0, 1))
    gains_got = swap(gains, "segment")
    gains_both = swap(gains_peer, "segment")
    other0 = give(own, 0)
    both0 = give(peer0, 0)
    square = ((512, 512), BF)
    layer_outs = [square, square, ((4, 128, 512), BF), ((4, 512, 128), BF)]
    gain = ((2, 512), F32)
    pair = ((2, 256, 256), BF)
    u0, v0, up0, down0, gains0, gains1, second0 = call(
        lambda ins, outs: weights_body(0, ins, outs),
        layer_outs + [gain, gain, pair],
        [],
        (
            own, peer0, other0, both0, two(second_mine), two(second_got),
            gains, gains_peer, gains_got, gains_both,
        ),
    )

    block = ((2, 256, 512), BF)
    next_msg, mixed0, x0, hidden0, middle = call(
        forward_cols_body,
        [tiles] + [block] * 4,
        [(MSG, F32)] * 3,
        (Near(msg), second0, gains0, gains1, u0, up0, down0, v0),
    )
    msg = send(next_msg)
    peer1 = swap_z(own, (1,))
    other1 = give(own, 1)
    first1, first1_t, second1, second1_t, second0_t = call(
        factors_body,
        [pair] * 5,
        [],
        (two(first_mine), two(first_got), two(second_mine), two(second_got)),
        after=(next_msg,),
    )
    (cot_tiles,) = call(pack_cot_body, [tiles], scratch_pack, (four(cot_rows),), after=(first1,))

    scratch_rows = [(MSG, F32), (MSG, F32), ((256, 128), F32), ((4, 256, 128), F32)]
    next_msg, scaled1 = call(
        rows_body, [Near((PAIR, BF)), block], scratch_rows, (Near(msg), first1, Near(cot_tiles))
    )
    msg = send(next_msg)
    both1 = give(peer1, 1)
    u1, v1, up1, down1 = call(
        lambda ins, outs: weights_body(1, ins, outs), layer_outs, [], (own, peer1, other1, both1)
    )
    next_msg, mixed1, back_turned1, direct = call(
        upper_cols_body,
        [tiles, block, block, ((2, 256, 512), F32)],
        [(MSG, F32)] * 3 + [((4, 256, 128), F32)],
        (Near(msg), second1, middle, gains1, v1, u1, up1, down1, second1_t),
    )
    msg = send(next_msg)

    halves = ((2, 2, 128, 256), BF)

    def channel_grad(outer, inner, after):
        (grad,) = call(grad_body, [halves], [], (outer, inner), after=(after,))
        return grad

    second_grad1 = channel_grad(back_turned1, mixed1, next_msg)

    (slopes,) = call(
        slope_body, [((2, 4, 256, 512), BF)], [], (hidden0, u0, up0), after=(second_grad1,)
    )

    next_msg, back_rows1 = call(
        rows_body, [tiles, block], scratch_rows, (Near(msg), first1_t, gains1)
    )
    msg = send(next_msg)
    first_grad1 = channel_grad(back_rows1, scaled1, next_msg)

    (x_sent,) = call(
        slice_body,
        [((2, 256, 256), BF)],
        [],
        ((rows, lambda ref: ref.at[pl.ds(2 * (2 * core() + 1 - side()), 2)], (2, 256, 256)),),
        after=(first_grad1,),
    )
    x_peer = swap(x_sent, "mp")

    next_msg, back_turned0 = call(
        lower_cols_body,
        [tiles, block],
        [(MSG, F32)] * 2,
        (
            Near(msg), part(direct, 0), v0, down0, part(slopes, 0), up0, u0, x0, gains0,
            part(direct, 1), part(slopes, 1), second0_t,
        ),
    )
    msg = send(next_msg)
    half = Near(((2, 128, 256), BF))
    mine, own_theirs, other_mine, other_theirs = call(
        second_grads_body,
        [half] * 4,
        [halves] * 2,
        (back_turned0, mixed0, second_grad1),
        after=(next_msg,),
    )
    from_side = swap(own_theirs, "mp")
    from_both = lax.ppermute(other_theirs, ("segment", "mp"), [(0, 3), (1, 2), (2, 1), (3, 0)])
    from_core = swap(other_mine, "segment")

    (message,) = call(
        last_rows_body,
        [Near(((4, 2, 128, 256), BF))],
        [(MSG, F32), ((4, 256, 128), F32)],
        (Near(msg), two(rows), x_peer, gains0, first_grad1),
    )
    grad_first = lax.all_to_all(message, ("segment", "mp"), split_axis=0, concat_axis=0, tiled=True)
    (grad_second,) = call(
        collect_body,
        [((8, 128, 256), F32)],
        [],
        (mine, from_core, from_side, from_both),
        after=(message,),
    )
    return grad_first.reshape(1, 8, 128, 256).astype(F32), grad_second[None]


def solution(mesh):
    placed = (
        P("seq", "mp"),
        P("seq", "mp"),
        P("segment", "mp"),
        P("segment", "mp"),
        P("segment", "seq", None, None),
        P("segment", "seq", None, None),
        P("segment", "mp", None, None),
        P("segment", "mp", None, None),
        P("segment", "mp", None, None),
        P("segment", "mp", None, None),
    )
    return jax.shard_map(
        layer_pair,
        mesh=mesh,
        in_specs=placed,
        out_specs=(P("segment", "seq", "mp", None), P("segment", "seq", "mp", None)),
        check_vma=False,
    )
```
